32 devices in a mesh: blk: 8 (over z, y), sub: 4 (over x, core).
Axes of the slice: x: 2, y: 2, z: 4, core: 2. Of those that a mesh axis runs over, the one named last changes fastest.
Arguments:
- pressure: float32 [2, 8, 8, 8, 16384], P(None, None, None, None, ('blk', 'sub')), may hold values from -6 to 6
- right_side: float32 [2, 8, 8, 8, 16384], P(None, None, None, None, ('blk', 'sub')), may hold values from -6 to 6
- geometry: float32 [6, 8, 8, 8, 16384], P(None, None, None, None, ('blk', 'sub')), may hold values from -0.03 to 0.08, as said below
- face_weight: float32 [64, 6, 16384], P(None, None, ('blk', 'sub')), may hold values from 0.004 to 0.02
- face_metric: float32 [64, 6, 16384], P(None, None, ('blk', 'sub')), may hold values from 0.5 to 2
- cross_slots: int32 [5, 32, 576], P(None, ('blk', 'sub')), may hold values from 0 to 511, as said below
- local_pairs: int32 [5, 16384], P(None, ('blk', 'sub')), may hold values from 0 to 511, as said below
- coarse_map: int32 [16384], P(('blk', 'sub')), may hold values from 0 to 255, as said below
- coarse_inverse: float32 [8, 8, 2048], P(None, None, 'blk'), may hold values from -0.12 to 0.48, as said below
Outputs:
- residual: float32 [2, 8, 8, 8, 16384], P(None, None, None, None, ('blk', 'sub'))
- corrected: float32 [2, 8, 8, 8, 16384], P(None, None, None, None, ('blk', 'sub'))
The draws below stay inside these ranges and needn't reach their ends.
Inputs may be any that keep to these rules, and one draw needn't show every extreme that they name: `cross_slots`: Rows: local element index, face 0 to 5 (low or high end of node axis 1, 2, 3), live flag, owner flag, orientation code 0 to 7. Columns come in 9 blocks of 64, block k for neighbour k of the device grid; block 4 (the device itself) has no live slot. The slot of device d at neighbour k, place c and the slot of neighbour k at column (8 - k) * 64 + c describe the same pair: equal live flags and codes, opposite owner flags. Within a block the live slots come first; every device shares exactly 64 pairs with some neighbour. Every (element, face) of a device appears at most once among its slots, live or not, and its local pairs. `local_pairs`: the columns of device d hold 512 pairs of its own elements; see cross_slots for the faces used. `coarse_map`: each coarse cell of a Morton block holds exactly 8 elements of that block. `geometry`: at each node the 3 x 3 matrix of the six rows is symmetric positive definite. `coarse_inverse`: each block is symmetric.
All inputs are finite; a program needn't handle non-finite values.
Results may differ from the reference program's by a relative error of at most 0.00016.
Values sent between devices are 32-bit elements; how exact they have to be, the bound alone decides.
No kernel may reach another device: no remote copies, remote signals or barrier semaphores. Data moves between devices by JAX's collectives and lax.ppermute only.
A program may use at most 128 MiB of HBM per device.

```python
import math
import jax
import jax.numpy as jnp
import numpy as np
from jax import lax

NP = 8
FACE = 64
FIELDS = 2
E_DEV = 512
RANKS = 32
ELEMS = 16384
CAP = 64
CROW = 256
CCELLS = 2048
N_SUB = 4


def pair_tables(key):
    base_key = jax.random.fold_in(key, 7)
    sub_keys = jax.random.split(base_key, 7)
    row_ids = jnp.arange(RANKS, dtype=jnp.int32)[:, None]
    direction = jnp.arange(9, dtype=jnp.int32)[None, :]
    block_place = row_ids // N_SUB
    sub_place = row_ids % N_SUB
    peer_rank = (block_place + direction // 3 - 1) % (RANKS // N_SUB) * N_SUB + (sub_place + direction % 3 - 1) % N_SUB
    mirror_dir = jnp.broadcast_to(8 - direction, (RANKS, 9))
    lower = direction < 4
    upper = direction > 4
    raw_counts = jax.random.randint(sub_keys[0], (RANKS, 9), 0, CAP + 1, dtype=jnp.int32)
    full_dir = jax.random.randint(sub_keys[1], (), 0, 4, dtype=jnp.int32)
    raw_counts = jnp.where(direction == full_dir, CAP, raw_counts)
    counts = jnp.where(lower, raw_counts, jnp.where(upper, raw_counts[peer_rank, mirror_dir], 0))
    slot_place = jnp.arange(CAP, dtype=jnp.int32)[None, None, :]
    live_flag = (slot_place < counts[:, :, None]).astype(jnp.int32)
    weights_dev = jax.random.randint(sub_keys[2], (RANKS,), 1, 9, dtype=jnp.int32)
    coin_draw = jax.random.randint(sub_keys[3], (RANKS, 9), 0, 1 << 20, dtype=jnp.int32)
    own_weight = jnp.broadcast_to(weights_dev[:, None], (RANKS, 9))
    upper_own = (coin_draw % (own_weight + weights_dev[peer_rank]) < own_weight).astype(jnp.int32)
    owner_flag = jnp.where(lower, upper_own, jnp.where(upper, 1 - upper_own[peer_rank, mirror_dir], 0))
    owner_flag = jnp.broadcast_to(owner_flag[:, :, None], (RANKS, 9, CAP))
    raw_codes = jax.random.randint(sub_keys[4], (RANKS, 9, CAP), 0, 8, dtype=jnp.int32)
    place_ids = jnp.broadcast_to(slot_place, (RANKS, 9, CAP))
    mirrored_codes = raw_codes[peer_rank[:, :, None], mirror_dir[:, :, None], place_ids]
    orient_codes = jnp.where(lower[:, :, None], raw_codes, mirrored_codes)
    face_ids = jax.vmap(lambda rank_id: jax.random.permutation(jax.random.fold_in(sub_keys[5], rank_id), 6 * E_DEV))(jnp.arange(RANKS, dtype=jnp.int32)).astype(jnp.int32)
    cross_ids = face_ids[:, :9 * CAP]
    local_ids = face_ids[:, 9 * CAP:9 * CAP + 2 * E_DEV].reshape(RANKS, E_DEV, 2)
    cross_table = jnp.stack([cross_ids % E_DEV, cross_ids // E_DEV, live_flag.reshape(RANKS, 9 * CAP), owner_flag.reshape(RANKS, 9 * CAP), orient_codes.reshape(RANKS, 9 * CAP)])
    local_codes = jax.random.randint(sub_keys[6], (RANKS, E_DEV), 0, 8, dtype=jnp.int32)
    local_table = jnp.stack([local_ids[:, :, 0] % E_DEV, local_ids[:, :, 0] // E_DEV, local_ids[:, :, 1] % E_DEV, local_ids[:, :, 1] // E_DEV, local_codes]).reshape(5, RANKS * E_DEV)
    return (cross_table.astype(jnp.int32), local_table.astype(jnp.int32))


def draw_cross_slots(key, part):
    return pair_tables(key)[0]


def draw_local_pairs(key, part):
    return pair_tables(key)[1]


def draw_coarse_map(key, part):
    cell_ids = jnp.arange(CROW * 8, dtype=jnp.int32) // 8
    blocks = jax.vmap(lambda row_index: jax.random.permutation(jax.random.fold_in(key, row_index), cell_ids))(jnp.arange(CCELLS // CROW, dtype=jnp.int32))
    return blocks.reshape(-1).astype(jnp.int32)


def draw_geometry(key, part):
    sub_keys = jax.random.split(key, 2)
    shape_all = (3, NP, NP, NP, ELEMS)
    diagonal = jnp.exp(jax.random.uniform(sub_keys[0], shape_all, jnp.float32, math.log(0.004), math.log(0.02)))
    coupling = jax.random.uniform(sub_keys[1], shape_all, jnp.float32, -0.3, 0.3)
    result = jnp.stack([diagonal[0], diagonal[1], diagonal[2], coupling[0] * jnp.sqrt(diagonal[0] * diagonal[1]), coupling[1] * jnp.sqrt(diagonal[0] * diagonal[2]), coupling[2] * jnp.sqrt(diagonal[1] * diagonal[2])])
    return result.astype(jnp.float32)


def draw_coarse_inverse(key, part):
    sub_keys = jax.random.split(key, 2)
    diagonal = jnp.exp(jax.random.uniform(sub_keys[0], (8, CCELLS), jnp.float32, math.log(0.04), math.log(0.12)))
    noise_draw = jax.random.uniform(sub_keys[1], (8, 8, CCELLS), jnp.float32, -0.03, 0.03)
    symmetric = 0.5 * (noise_draw + jnp.transpose(noise_draw, (1, 0, 2)))
    identity = jnp.eye(8, dtype=jnp.float32)[:, :, None]
    blocks = symmetric * (1.0 - identity) + identity * diagonal[:, None, :]
    return blocks.astype(jnp.float32)


def block_scale(own_key, extent, pieces, smallest, top_value):
    def one(axis_at, parts):
        heights = jax.random.uniform(jax.random.fold_in(jax.random.fold_in(own_key, 6), axis_at), (parts,), jnp.float32, smallest / len(pieces), top_value / len(pieces))
        return jnp.repeat(jnp.exp(heights), extent[axis_at] // parts).reshape((-1,) + (1,) * (len(extent) - axis_at - 1))

    level = one(*pieces[0])
    for cut in pieces[1:]:
        level = level * one(*cut)
    return level


def gaussian(rng, extent, width, limit, shards=(), held_as=jnp.bfloat16):
    values = jax.random.normal(rng, extent, jnp.float32) * width
    if len(shards) > 0:
        values = block_scale(rng, extent, shards, -0.22, 0.18) * values
    return jnp.clip(values, min=-limit, max=limit).astype(held_as)


def setup_inputs(seed: int = 0) -> dict:
    key_list = jax.random.split(jax.random.key(seed), 10)
    pressure = gaussian(key_list[0], (FIELDS, NP, NP, NP, ELEMS), 1.0, 6.0, ((4, 32),), jnp.float32)
    right_side = gaussian(key_list[1], (FIELDS, NP, NP, NP, ELEMS), 1.0, 6.0, ((4, 32),), jnp.float32)
    geometry = draw_geometry(jax.random.fold_in(key_list[9], 71), 0)
    face_weight = jnp.clip(jnp.exp(math.log(0.02) - 1.6094378 * jax.random.uniform(key_list[3], (FACE, 6, ELEMS), jnp.float32) ** block_scale(key_list[3], (FACE, 6, ELEMS), ((2, 32),), -0.2, 0.2)), 0.004, 0.02)
    face_metric = jnp.clip(jnp.exp(math.log(2.0) - 1.3862944 * jax.random.uniform(key_list[4], (FACE, 6, ELEMS), jnp.float32) ** block_scale(key_list[4], (FACE, 6, ELEMS), ((2, 32),), -0.2, 0.2)), 0.5, 2.0)
    cross_slots = draw_cross_slots(jax.random.fold_in(key_list[9], 71), 0)
    local_pairs = draw_local_pairs(jax.random.fold_in(key_list[9], 71), 0)
    coarse_map = draw_coarse_map(jax.random.fold_in(key_list[9], 71), 0)
    coarse_inverse = draw_coarse_inverse(jax.random.fold_in(key_list[9], 71), 0)
    return {"pressure": pressure, "right_side": right_side, "geometry": geometry, "face_weight": face_weight, "face_metric": face_metric, "cross_slots": cross_slots, "local_pairs": local_pairs, "coarse_map": coarse_map, "coarse_inverse": coarse_inverse}


precise = lax.Precision.HIGHEST


def node_points(node_count):
    if node_count == 8:
        positive = [0.2092992179024789, 0.5917001814331423, 0.8717401485096066, 1.0]
    else:
        positive = [0.4472135954999579, 1.0]
    return np.array(sorted([-entry_value for entry_value in positive] + positive))


def derivative_matrix(node_count):
    points = node_points(node_count)
    weights = np.array([1.0 / np.prod([points[row_index] - points[col_index] for col_index in range(node_count) if col_index != row_index]) for row_index in range(node_count)])
    matrix = np.zeros((node_count, node_count))
    for row_index in range(node_count):
        for col_index in range(node_count):
            if row_index != col_index:
                matrix[row_index, col_index] = weights[col_index] / weights[row_index] / (points[row_index] - points[col_index])
        matrix[row_index, row_index] = -np.sum(matrix[row_index])
    return matrix


def edge_matrix(node_count):
    derivative = derivative_matrix(node_count)
    edge_rows = np.zeros((4, node_count))
    edge_rows[0, 0] = 1.0
    edge_rows[1] = -derivative[0]
    edge_rows[2, node_count - 1] = 1.0
    edge_rows[3] = derivative[node_count - 1]
    return edge_rows


def prolong_matrix(node_count):
    points = node_points(node_count)
    return np.stack([(1.0 - points) / 2.0, (1.0 + points) / 2.0], axis=1)


def orient_tables(node_count):
    forward = np.zeros((8, node_count * node_count), np.int32)
    for orient_code in range(8):
        for first_axis in range(node_count):
            for second_axis in range(node_count):
                if orient_code & 4:
                    source_one, source_two = second_axis, first_axis
                else:
                    source_one, source_two = first_axis, second_axis
                if orient_code & 1:
                    source_one = node_count - 1 - source_one
                if orient_code & 2:
                    source_two = node_count - 1 - source_two
                forward[orient_code, first_axis * node_count + second_axis] = source_one * node_count + source_two
    inverse = np.argsort(forward, axis=1).astype(np.int32)
    return forward, inverse


def reorient(traces, orient_codes, table):
    result = jnp.zeros_like(traces)
    for orient_code in range(8):
        permuted = jnp.take(traces, jnp.asarray(table[orient_code], jnp.int32), axis=-2)
        result = result + jnp.where(orient_codes == orient_code, permuted, 0.0)
    return result


def face_flux(first_side, second_side, orient_codes, node_count):
    forward, inverse = orient_tables(node_count)
    first_value, first_slope, first_weight, first_metric = first_side
    second_value = reorient(second_side[0], orient_codes, forward)
    second_slope = reorient(second_side[1], orient_codes, forward)
    second_weight = reorient(second_side[2], orient_codes, forward)
    second_metric = reorient(second_side[3], orient_codes, forward)
    penalty = node_count * (node_count + 1) / 2.0
    jump_value = first_value - second_value
    weight = 0.5 * (first_weight + second_weight)
    penalty_term = penalty * 0.5 * (first_metric + second_metric)
    normal_term = weight * (penalty_term * jump_value - 0.5 * (first_slope - second_slope))
    symmetric_term = -0.5 * weight * jump_value
    return (normal_term, symmetric_term * first_metric,
            -reorient(normal_term, orient_codes, inverse),
            -reorient(symmetric_term, orient_codes, inverse) * second_side[3])


def volume_term(fields, geometry, derivative):
    deriv_table = jnp.asarray(derivative, jnp.float32)
    slope_first = jnp.einsum('ik,fkjle->fijle', deriv_table, fields, precision=precise)
    slope_second = jnp.einsum('jk,fikle->fijle', deriv_table, fields, precision=precise)
    slope_third = jnp.einsum('lk,fijke->fijle', deriv_table, fields, precision=precise)
    flux_first = geometry[0] * slope_first + geometry[3] * slope_second + geometry[4] * slope_third
    flux_second = geometry[3] * slope_first + geometry[1] * slope_second + geometry[5] * slope_third
    flux_third = geometry[4] * slope_first + geometry[5] * slope_second + geometry[2] * slope_third
    result = jnp.einsum('ki,fkjle->fijle', deriv_table, flux_first, precision=precise)
    result = result + jnp.einsum('kj,fikle->fijle', deriv_table, flux_second, precision=precise)
    return result + jnp.einsum('kl,fijke->fijle', deriv_table, flux_third, precision=precise)


def face_traces(fields, face_metric, edge_rows):
    field_count = fields.shape[0]
    elem_count = fields.shape[-1]
    face_size = fields.shape[1] * fields.shape[1]
    einsum_forms = ['ak,fkjle->fajle', 'ak,fikle->faile', 'ak,fijke->faije']
    values = []
    slopes = []
    for einsum_form in einsum_forms:
        along_axis = jnp.einsum(einsum_form, edge_rows, fields, precision=precise)
        flat_rows = along_axis.reshape(field_count, 4, face_size, elem_count)
        values += [flat_rows[:, 0], flat_rows[:, 2]]
        slopes += [flat_rows[:, 1], flat_rows[:, 3]]
    value_all = jnp.stack(values, axis=2)
    slope_all = jnp.stack(slopes, axis=2) * face_metric
    return value_all.reshape(field_count, face_size, 6 * elem_count), slope_all.reshape(field_count, face_size, 6 * elem_count)


def lift_faces(value_sum, lift_sum, edge_rows, node_count):
    field_count, face_size, flat_count = value_sum.shape
    elem_count = flat_count // 6
    value_grid = value_sum.reshape(field_count, face_size, 6, elem_count)
    lift_grid = lift_sum.reshape(field_count, face_size, 6, elem_count)
    einsum_forms = ['ak,fajle->fkjle', 'ak,faile->fikle', 'ak,faije->fijke']
    result = 0.0
    for axis_number, einsum_form in enumerate(einsum_forms):
        stacked = jnp.stack([value_grid[:, :, 2 * axis_number], lift_grid[:, :, 2 * axis_number],
                             value_grid[:, :, 2 * axis_number + 1], lift_grid[:, :, 2 * axis_number + 1]], axis=1)
        stacked = stacked.reshape(field_count, 4, node_count, node_count, elem_count)
        result = result + jnp.einsum(einsum_form, edge_rows, stacked, precision=precise)
    return result


def deposit(running, slot_index, contribution, weight_mask):
    return running.at[:, :, slot_index].add(contribution * weight_mask)


def restrict(residual, prolong):
    coarse = jnp.einsum('ia,jb,kc,fijke->fabce', prolong, prolong, prolong, residual, precision=precise)
    return coarse.reshape(residual.shape[0], 8, residual.shape[-1])


def prolong_back(coarse, prolong):
    shaped = coarse.reshape(coarse.shape[0], 2, 2, 2, coarse.shape[-1])
    return jnp.einsum('ia,jb,kc,fabce->fijke', prolong, prolong, prolong, shaped, precision=precise)


def reference(pressure, right_side, geometry, face_weight, face_metric, cross_slots, local_pairs, coarse_map, coarse_inverse):
    derivative = derivative_matrix(NP)
    edge_rows = jnp.asarray(edge_matrix(NP), jnp.float32)
    volume = lax.map(lambda single: volume_term(single[None], geometry, derivative)[0], pressure)
    value_all, slope_all = face_traces(pressure, face_metric, edge_rows)
    weight_flat = face_weight.reshape(FACE, 6 * ELEMS)
    metric_flat = face_metric.reshape(FACE, 6 * ELEMS)

    def select_side(slot_index):
        return (jnp.take(value_all, slot_index, axis=2), jnp.take(slope_all, slot_index, axis=2),
                jnp.take(weight_flat, slot_index, axis=1), jnp.take(metric_flat, slot_index, axis=1))

    device_rank = jnp.arange(RANKS, dtype=jnp.int32)[:, None]
    slot_column = jnp.arange(9 * CAP, dtype=jnp.int32)[None, :]
    direction = slot_column // CAP
    block_place = device_rank // N_SUB
    sub_place = device_rank % N_SUB
    peer_rank = ((block_place + direction // 3 - 1) % (RANKS // N_SUB)) * N_SUB + (sub_place + direction % 3 - 1) % N_SUB
    mirror = (8 - direction) * CAP + slot_column % CAP
    second_elem = cross_slots[0][peer_rank, mirror]
    second_face = cross_slots[1][peer_rank, mirror]
    first_index = (cross_slots[1] * ELEMS + device_rank * E_DEV + cross_slots[0]).reshape(-1)
    second_index = (second_face * ELEMS + peer_rank * E_DEV + second_elem).reshape(-1)
    own_mask = (cross_slots[2] * cross_slots[3]).reshape(-1).astype(jnp.float32)
    orient_codes = cross_slots[4].reshape(-1)
    first_value, first_lift, second_value, second_lift = face_flux(select_side(first_index), select_side(second_index), orient_codes, NP)
    value_sum = jnp.zeros((FIELDS, FACE, 6 * ELEMS), jnp.float32)
    lift_sum = jnp.zeros((FIELDS, FACE, 6 * ELEMS), jnp.float32)
    value_sum = deposit(value_sum, first_index, first_value, own_mask)
    value_sum = deposit(value_sum, second_index, second_value, own_mask)
    lift_sum = deposit(lift_sum, first_index, first_lift, own_mask)
    lift_sum = deposit(lift_sum, second_index, second_lift, own_mask)
    local_rank = jnp.arange(ELEMS, dtype=jnp.int32) // E_DEV
    local_first = local_pairs[1] * ELEMS + local_rank * E_DEV + local_pairs[0]
    local_second = local_pairs[3] * ELEMS + local_rank * E_DEV + local_pairs[2]
    first_value, first_lift, second_value, second_lift = face_flux(select_side(local_first), select_side(local_second), local_pairs[4], NP)
    value_sum = deposit(value_sum, local_first, first_value, 1.0)
    value_sum = deposit(value_sum, local_second, second_value, 1.0)
    lift_sum = deposit(lift_sum, local_first, first_lift, 1.0)
    lift_sum = deposit(lift_sum, local_second, second_lift, 1.0)
    operated = volume + lift_faces(value_sum, lift_sum, edge_rows, NP)
    residual = right_side - operated
    prolong = jnp.asarray(prolong_matrix(NP), jnp.float32)
    restricted = restrict(residual, prolong)
    cell_ids = (jnp.arange(ELEMS, dtype=jnp.int32) // (8 * CROW)) * CROW + coarse_map
    cell_sums = jax.ops.segment_sum(jnp.moveaxis(restricted, 2, 0), cell_ids, num_segments=CCELLS)
    correction = jnp.einsum('ijc,cfj->cfi', coarse_inverse, cell_sums, precision=precise)
    spread = jnp.moveaxis(correction[cell_ids], 0, 2)
    corrected = pressure + prolong_back(spread, prolong)
    return residual, corrected
```

```python
import functools

import jax
import jax.numpy as jnp
import numpy as np
from jax import lax
from jax.experimental import pallas as pl
from jax.experimental.pallas import tpu as pltpu
from jax.sharding import PartitionSpec as P


LANES = 128
MIB = 1024 * 1024


def node_points():
    positive = [0.2092992179024789, 0.5917001814331423, 0.8717401485096066, 1.0]
    return np.array(sorted([-entry for entry in positive] + positive))


def derivative_matrix(node_count):
    points = node_points()
    weights = np.array(
        [
            1.0 / np.prod([points[row] - points[col] for col in range(node_count) if col != row])
            for row in range(node_count)
        ]
    )
    matrix = np.zeros((node_count, node_count))
    for row in range(node_count):
        for col in range(node_count):
            if row != col:
                matrix[row, col] = weights[col] / weights[row] / (points[row] - points[col])
        matrix[row, row] = -np.sum(matrix[row])
    return matrix


def inverse_code(code):
    swapped = 4 + 2 * jnp.bitwise_and(code, 1) + jnp.bitwise_and(jnp.right_shift(code, 1), 1)
    return jnp.where(code >= 4, swapped, code)


def spread_down(row):
    return jnp.broadcast_to(row, (LANES, LANES)).T


def lane_order(code, nodes):
    lane = lax.broadcasted_iota(jnp.int32, code.shape, 1)
    half = nodes * nodes
    place = jnp.bitwise_and(lane, half - 1)
    one, two = place // nodes, jnp.bitwise_and(place, nodes - 1)
    other = lane - place + two * nodes + one
    first = jnp.bitwise_and(code, 1) * ((nodes - 1) * nodes)
    second = jnp.bitwise_and(jnp.right_shift(code, 1), 1) * (nodes - 1)
    return jnp.bitwise_xor(jnp.where(jnp.bitwise_and(code, 4) > 0, other, lane), first + second)


def column(values):
    place = lax.broadcasted_iota(jnp.int32, (len(values), LANES), 0)
    result = jnp.full((len(values), LANES), float(values[0]), jnp.float32)
    for at, value in enumerate(values[1:], 1):
        result = jnp.where(place == at, float(value), result)
    return result


def weighted(factors, terms):
    running = None
    for factor, term in zip(factors, terms):
        if float(factor) == 0.0:
            continue
        product = term if float(factor) == 1.0 else float(factor) * term
        running = product if running is None else running + product
    return running


def derive(matrix, terms):
    count = len(terms)
    half = count // 2
    even = [terms[k] + terms[count - 1 - k] for k in range(half)]
    odd = [terms[k] - terms[count - 1 - k] for k in range(half)]
    low, high = [], []
    for i in range(half):
        plus = weighted([0.5 * (matrix[i, k] + matrix[i, count - 1 - k]) for k in range(half)], even)
        minus = weighted([0.5 * (matrix[i, k] - matrix[i, count - 1 - k]) for k in range(half)], odd)
        low.append(minus + plus)
        high.append(minus - plus)
    return low + high[::-1]


def split(value):
    head = value.astype(jnp.bfloat16)
    return head, (value - head.astype(jnp.float32)).astype(jnp.bfloat16)


def mxu(left, right, dims=(((1,), (0,)), ((), ()))):
    return lax.dot_general(left, right, dims, preferred_element_type=jnp.float32)


def trace_kernel(rows_ref, p_ref, fw_ref, fm_ref, table, send_ref, nat, *, derivative, elems):
    step = pl.program_id(0)
    steps = pl.num_programs(0)
    fields, nodes = p_ref.shape[0], p_ref.shape[1]
    pieces_total = fields + 1
    face_size = nodes * nodes
    last = nodes - 1
    flat = p_ref.reshape(fields * nodes * nodes * nodes, LANES)
    base = step * LANES
    low = [-derivative[0, k] for k in range(nodes)]
    high = [derivative[last, k] for k in range(nodes)]

    def put(face, piece, part):
        table[pl.ds((face * elems + base) * pieces_total + piece, LANES, stride=pieces_total), :] = part.T

    for face in range(6):
        put(face, fields, jnp.concatenate([fw_ref[face], fm_ref[face]], axis=0))

    for f in range(fields):
        for axis in range(3):
            for at in range(nodes):
                if axis == 0:
                    terms = [p_ref[f, k, at] for k in range(nodes)]
                elif axis == 1:
                    terms = [p_ref[f, at, k] for k in range(nodes)]
                else:
                    first = (f * nodes + at) * nodes * nodes
                    terms = [flat[pl.ds(first + k, nodes, stride=nodes), :] for k in range(nodes)]
                rows = slice(at * nodes, (at + 1) * nodes)
                more = slice(face_size + at * nodes, face_size + (at + 1) * nodes)
                nat[f, 2 * axis, rows] = terms[0]
                nat[f, 2 * axis, more] = weighted(low, terms)
                nat[f, 2 * axis + 1, rows] = terms[last]
                nat[f, 2 * axis + 1, more] = weighted(high, terms)
            put(2 * axis, f, nat[f, 2 * axis])
            put(2 * axis + 1, f, nat[f, 2 * axis + 1])

    @pl.when(step == steps - 1)
    def _():
        group_size = 16
        slot_total = send_ref.shape[0] // pieces_total

        def pick(group, carry):
            for u in range(group_size):
                k = group * group_size + u
                send_ref[pl.ds(k * pieces_total, pieces_total), :] = table[pl.ds(rows_ref[k], pieces_total), :]
            return carry

        lax.fori_loop(0, slot_total // group_size, pick, 0)


def traces(rows, pressure, face_weight, face_metric, derivative):
    fields, nodes, elems = pressure.shape[0], pressure.shape[1], pressure.shape[-1]
    face_size = nodes * nodes
    slot_total = rows.shape[0]
    face_spec = pl.BlockSpec((6, face_size, LANES), lambda s: (0, 0, s))
    whole = pl.BlockSpec(memory_space=pltpu.VMEM)
    return pl.pallas_call(
        functools.partial(trace_kernel, derivative=derivative, elems=elems),
        out_shape=(
            jax.ShapeDtypeStruct((6 * elems * (fields + 1), LANES), jnp.float32),
            jax.ShapeDtypeStruct((slot_total * (fields + 1), LANES), jnp.float32),
        ),
        grid=(elems // LANES,),
        in_specs=[
            pl.BlockSpec(memory_space=pltpu.SMEM),
            pl.BlockSpec((fields, nodes, nodes, nodes, LANES), lambda s: (0, 0, 0, 0, s)),
            face_spec,
            face_spec,
        ],
        out_specs=(whole, whole),
        scratch_shapes=[pltpu.VMEM((fields, 6, 2 * face_size, LANES), jnp.float32)],
        compiler_params=pltpu.CompilerParams(vmem_limit_bytes=16 * MIB),
        cost_estimate=pl.CostEstimate(flops=10**7, bytes_accessed=9 * 10**6, transcendentals=0),
        name="traces",
    )(rows, pressure, face_weight, face_metric)


def flux_rows(own, other, order, fields, nodes):
    half = nodes * nodes
    penalty = nodes * (nodes + 1) / 2.0
    lane = lax.broadcasted_iota(jnp.int32, order.shape, 1)
    head = lane < half
    turned = [jnp.take_along_axis(piece, order, axis=1) for piece in other]
    own_wm, other_wm = own[fields], turned[fields]
    mean = 0.5 * (own_wm + other_wm)
    swapped = pltpu.roll(mean, half, 1)
    weight = jnp.where(head, mean, swapped)
    own_scale = jnp.where(head, 1.0, own_wm)
    other_scale = jnp.where(head, 1.0, other_wm)
    direct = jnp.where(head, penalty * weight * swapped, 0.0)
    crossed = -0.5 * weight * own_scale
    results = []
    for f in range(fields):
        gap = own[f] * own_scale - turned[f] * other_scale
        results.append(direct * gap + crossed * pltpu.roll(gap, half, 1))
    return results


def pieces(ref, start, rows, fields):
    return [ref[pl.ds(start * (fields + 1) + f, rows, stride=fields + 1), :] for f in range(fields + 1)]


def local_kernel(from_ref, to_ref, code_ref, table_ref, out_ref, picked, order, result, *, fields, nodes):
    total = from_ref.shape[0]
    count = total // 2
    width = fields + 1
    group_size = 16
    out_ref[...] = jnp.zeros_like(out_ref)

    def pick(group, carry):
        for u in range(group_size):
            k = group * group_size + u
            picked[pl.ds(k * width, width), :] = table_ref[pl.ds(from_ref[k], width), :]
        return carry

    lax.fori_loop(0, total // group_size, pick, 0)
    for at in range(count // LANES):
        code = code_ref[4:5, at * LANES : (at + 1) * LANES]
        column_code = spread_down(code.astype(jnp.float32)).astype(jnp.int32)
        order[at * LANES : (at + 1) * LANES, :] = lane_order(column_code, nodes)
        order[count + at * LANES : count + (at + 1) * LANES, :] = lane_order(inverse_code(column_code), nodes)
    rows = 32

    def flux(at, carry):
        start = at * rows
        other = lax.rem(start + count, total)
        values = flux_rows(
            pieces(picked, start, rows, fields),
            pieces(picked, other, rows, fields),
            order[pl.ds(pl.multiple_of(start, rows), rows), :],
            fields,
            nodes,
        )
        for f in range(fields):
            result[pl.ds(start * fields + f, rows, stride=fields), :] = values[f]
        return carry

    lax.fori_loop(0, total // rows, flux, 0)

    def place(group, carry):
        for u in range(group_size):
            k = group * group_size + u
            out_ref[pl.ds(to_ref[k], fields), :] = result[pl.ds(k * fields, fields), :]
        return carry

    lax.fori_loop(0, total // group_size, place, 0)


def local_fluxes(rows_from, rows_to, local_pairs, table, fields, nodes, elems):
    total = rows_from.shape[0]
    vmem = pl.BlockSpec(memory_space=pltpu.VMEM)
    smem = pl.BlockSpec(memory_space=pltpu.SMEM)
    return pl.pallas_call(
        functools.partial(local_kernel, fields=fields, nodes=nodes),
        out_shape=jax.ShapeDtypeStruct((6 * elems * fields, LANES), jnp.float32),
        in_specs=[smem, smem, vmem, vmem],
        out_specs=vmem,
        scratch_shapes=[
            pltpu.VMEM((total * (fields + 1), LANES), jnp.float32),
            pltpu.VMEM((total, LANES), jnp.int32),
            pltpu.VMEM((total * fields, LANES), jnp.float32),
        ],
        compiler_params=pltpu.CompilerParams(vmem_limit_bytes=16 * MIB),
        cost_estimate=pl.CostEstimate(flops=10**7, bytes_accessed=12 * 10**6, transcendentals=0),
        name="local_fluxes",
    )(rows_from, rows_to, local_pairs, table)


def volume_kernel(p_ref, rs_ref, g_ref, dh_ref, dl_ref, th_ref, tl_ref, out_ref, one, two, three, *, derivative):
    fields, nodes = p_ref.shape[0], p_ref.shape[1]
    rows = nodes**3
    block = dh_ref.shape[0]
    back = derivative.T

    def along_last(read, write, head_ref, tail_ref):
        for at in range(rows // block):
            value = jnp.concatenate([read(f)[at * block : (at + 1) * block] for f in range(fields)], axis=1)
            head, tail = split(value)
            result = mxu(head_ref[...], head) + mxu(head_ref[...], tail) + mxu(tail_ref[...], head)
            for f in range(fields):
                write(f, at, result[:, f * LANES : (f + 1) * LANES])

    def put_three(f, at, value):
        three[f, at * (block // 64) : (at + 1) * (block // 64)] = value.reshape(block // 64, nodes, nodes, LANES)

    along_last(lambda f: p_ref[f].reshape(rows, LANES), put_three, dh_ref, dl_ref)
    for f in range(fields):
        for j in range(nodes):
            slopes = derive(derivative, [p_ref[f, k, j] for k in range(nodes)])
            for i in range(nodes):
                one[f, i, j] = slopes[i]
    for i in range(nodes):
        for f in range(fields):
            slopes = derive(derivative, [p_ref[f, i, k] for k in range(nodes)])
            flux = []
            for j in range(nodes):
                s1, s2, s3 = one[f, i, j], slopes[j], three[f, i, j]
                xx, yy, zz, xy, xz, yz = [g_ref[c, i, j] for c in range(6)]
                one[f, i, j] = xx * s1 + xy * s2 + xz * s3
                flux.append(xy * s1 + yy * s2 + yz * s3)
                three[f, i, j] = xz * s1 + yz * s2 + zz * s3
            for j, value in enumerate(derive(back, flux)):
                two[f, i, j] = rs_ref[f, i, j] - value

    def put_two(f, at, value):
        part = value.reshape(block // 64, nodes, nodes, LANES)
        rng = slice(at * (block // 64), (at + 1) * (block // 64))
        two[f, rng] = two[f, rng] - part

    along_last(lambda f: three[f].reshape(rows, LANES), put_two, th_ref, tl_ref)
    for f in range(fields):
        for j in range(nodes):
            sums = derive(back, [one[f, k, j] for k in range(nodes)])
            for i in range(nodes):
                out_ref[f, i, j] = two[f, i, j] - sums[i]


def volume(pressure, right_side, geometry, derivative):
    fields, nodes, elems = pressure.shape[0], pressure.shape[1], pressure.shape[-1]
    block = 256
    spread = np.kron(np.eye(block // nodes), derivative)

    def parts(matrix):
        head = jnp.asarray(matrix, jnp.float32).astype(jnp.bfloat16)
        tail = (jnp.asarray(matrix, jnp.float32) - head.astype(jnp.float32)).astype(jnp.bfloat16)
        return head, tail

    whole = (fields, nodes, nodes, nodes, LANES)
    field_spec = pl.BlockSpec(whole, lambda s: (0, 0, 0, 0, s))
    table_spec = pl.BlockSpec((block, block), lambda s: (0, 0))
    return pl.pallas_call(
        functools.partial(volume_kernel, derivative=derivative),
        out_shape=jax.ShapeDtypeStruct(pressure.shape, jnp.float32),
        grid=(elems // LANES,),
        in_specs=[
            field_spec,
            field_spec,
            pl.BlockSpec((6, nodes, nodes, nodes, LANES), lambda s: (0, 0, 0, 0, s)),
            table_spec,
            table_spec,
            table_spec,
            table_spec,
        ],
        out_specs=field_spec,
        scratch_shapes=[pltpu.VMEM(whole, jnp.float32)] * 3,
        compiler_params=pltpu.CompilerParams(vmem_limit_bytes=16 * MIB),
        cost_estimate=pl.CostEstimate(flops=10**9, bytes_accessed=13 * 10**6, transcendentals=0),
        name="volume",
    )(pressure, right_side, geometry, *parts(spread), *parts(spread.T))


def residual_kernel(
    to_ref, slots_ref, own_ref, got0, got1, got2, got3, got4, got5, got6, got7, start_ref, rows_in, map_ref,
    res_ref, sums_ref, rows_ref, order, result, nat, restricted,
    *, derivative, prolong, elems, fields, nodes,
):
    step = pl.program_id(0)
    slot_total = to_ref.shape[0]
    cap = slot_total // 9
    half = nodes * nodes
    last = nodes - 1
    del rows_in

    @pl.when(step == 0)
    def _():
        source = dict(zip((0, 1, 2, 3, 5, 6, 7, 8), (got0, got1, got2, got3, got4, got5, got6, got7)))
        code = jnp.where(slots_ref[3] > 0, slots_ref[4], inverse_code(slots_ref[4]))
        flags = (code + 8 * slots_ref[2]).astype(jnp.float32)
        flags = jnp.concatenate([flags, jnp.zeros((1, order.shape[0] - slot_total), jnp.float32)], axis=1)
        for at in range(order.shape[0] // LANES):
            order[at * LANES : (at + 1) * LANES, :] = spread_down(flags[:, at * LANES : (at + 1) * LANES]).astype(
                jnp.int32
            )
        result[4 * cap * fields : 5 * cap * fields, :] = jnp.zeros((cap * fields, LANES), jnp.float32)
        rows = min(cap, 32)
        for k, ref in source.items():
            for part in range(cap // rows):
                first = k * cap + part * rows
                flag = order[first : first + rows, :]
                values = flux_rows(
                    pieces(own_ref, first, rows, fields),
                    pieces(ref, part * rows, rows, fields),
                    lane_order(flag, nodes),
                    fields,
                    nodes,
                )
                for f in range(fields):
                    result[pl.ds(first * fields + f, rows, stride=fields), :] = jnp.where(flag >= 8, values[f], 0.0)
        group_size = 16

        def put(group, carry):
            for u in range(group_size):
                k = group * group_size + u
                rows_ref[pl.ds(to_ref[k], fields), :] = result[pl.ds(k * fields, fields), :]
            return carry

        lax.fori_loop(0, slot_total // group_size, put, 0)

    base = step * LANES
    for f in range(fields):
        for face in range(6):
            nat[f, face] = rows_ref[pl.ds((face * elems + base) * fields + f, LANES, stride=fields), :].T
    value_low = column([1.0] + [0.0] * last)
    value_high = column([0.0] * last + [1.0])
    lift_low = column(list(-derivative[0]))
    lift_high = column(list(derivative[last]))
    ramp = prolong[:, 1]
    ramp_rows = column(list(ramp))
    for f in range(fields):
        spots = [[None, None], [None, None]]
        for i in range(nodes):
            pencil = []
            for j in range(nodes):
                value = start_ref[f, i, j]
                at_j = slice(j * nodes, (j + 1) * nodes)
                at_i = slice(i * nodes, (i + 1) * nodes)
                low_j = slice(half + j * nodes, half + (j + 1) * nodes)
                low_i = slice(half + i * nodes, half + (i + 1) * nodes)
                if i == 0:
                    value = value - nat[f, 0, at_j]
                if i == last:
                    value = value - nat[f, 1, at_j]
                value = value + float(derivative[0, i]) * nat[f, 0, low_j]
                value = value - float(derivative[last, i]) * nat[f, 1, low_j]
                if j == 0:
                    value = value - nat[f, 2, at_i]
                if j == last:
                    value = value - nat[f, 3, at_i]
                value = value + float(derivative[0, j]) * nat[f, 2, low_i]
                value = value - float(derivative[last, j]) * nat[f, 3, low_i]
                node = i * nodes + j
                value = value - value_low * nat[f, 4, node : node + 1]
                value = value - lift_low * nat[f, 4, half + node : half + node + 1]
                value = value - value_high * nat[f, 5, node : node + 1]
                value = value - lift_high * nat[f, 5, half + node : half + node + 1]
                res_ref[f, i, j] = value
                pencil.append(value)
            total = weighted([1.0] * nodes, pencil)
            sloped = weighted(list(ramp), pencil)
            for b, part in enumerate((total, sloped)):
                spots[0][b] = part if i == 0 else spots[0][b] + part
                extra = float(ramp[i]) * part
                if float(ramp[i]) != 0.0:
                    spots[1][b] = extra if spots[1][b] is None else spots[1][b] + extra
        for a in range(2):
            for b in range(2):
                if a == 0:
                    part = spots[0][b] - spots[1][b]
                    other = spots[0][1] - spots[1][1]
                else:
                    part = spots[1][b]
                    other = spots[1][1]
                if b == 0:
                    part = part - other
                whole = jnp.sum(part, axis=0, keepdims=True)
                up = jnp.sum(part * ramp_rows, axis=0, keepdims=True)
                at = f * 8 + 4 * a + 2 * b
                restricted[at : at + 1, :] = whole - up
                restricted[at + 1 : at + 2, :] = up

    cells = sums_ref.shape[1]
    hot = (lax.broadcasted_iota(jnp.int32, (cells, LANES), 0) == map_ref[...]).astype(jnp.bfloat16)
    value = restricted[...]
    head, rest = split(value)
    tail = (value - head.astype(jnp.float32) - rest.astype(jnp.float32)).astype(jnp.bfloat16)
    across = (((1,), (1,)), ((), ()))
    sums = mxu(head, hot, across) + mxu(rest, hot, across) + mxu(tail, hot, across)

    @pl.when(step == 0)
    def _():
        sums_ref[...] = sums

    @pl.when(step > 0)
    def _():
        sums_ref[...] += sums


def residuals(rows_to, slots, own, received, start, local_rows, cell_row, cells, derivative, prolong):
    fields, nodes, elems = start.shape[0], start.shape[1], start.shape[-1]
    slot_total = rows_to.shape[0]
    padded = -(-slot_total // LANES) * LANES
    field_spec = pl.BlockSpec((fields, nodes, nodes, nodes, LANES), lambda s: (0, 0, 0, 0, s))
    vmem = pl.BlockSpec(memory_space=pltpu.VMEM)
    residual, sums, _ = pl.pallas_call(
        functools.partial(
            residual_kernel, derivative=derivative, prolong=prolong, elems=elems, fields=fields, nodes=nodes
        ),
        out_shape=(
            jax.ShapeDtypeStruct(start.shape, jnp.float32),
            jax.ShapeDtypeStruct((fields * 8, cells), jnp.float32),
            jax.ShapeDtypeStruct(local_rows.shape, jnp.float32),
        ),
        grid=(elems // LANES,),
        in_specs=[pl.BlockSpec(memory_space=pltpu.SMEM)] + [vmem] * 10
        + [field_spec, vmem, pl.BlockSpec((1, LANES), lambda s: (0, s))],
        out_specs=(field_spec, pl.BlockSpec((fields * 8, cells), lambda s: (0, 0)), vmem),
        scratch_shapes=[
            pltpu.VMEM((padded, LANES), jnp.int32),
            pltpu.VMEM((slot_total * fields, LANES), jnp.float32),
            pltpu.VMEM((fields, 6, LANES, LANES), jnp.float32),
            pltpu.VMEM((fields * 8, LANES), jnp.float32),
        ],
        input_output_aliases={12: 2},
        compiler_params=pltpu.CompilerParams(vmem_limit_bytes=16 * MIB),
        cost_estimate=pl.CostEstimate(flops=10**8, bytes_accessed=9 * 10**6, transcendentals=0),
        name="residuals",
    )(rows_to, slots, own, *received, start, local_rows, cell_row)
    return residual, sums


def correct_kernel(p_ref, inverse_ref, map_ref, *refs, prolong, parts):
    sum_refs = refs[:parts]
    out_ref, heads, rests, tails = refs[parts:]
    step = pl.program_id(0)
    fields, nodes = p_ref.shape[0], p_ref.shape[1]
    cells = inverse_ref.shape[-1]

    @pl.when(step == 0)
    def _():
        total = sum_refs[0][...]
        for ref in sum_refs[1:]:
            total = total + ref[...]
        for f in range(fields):
            running = None
            for j in range(8):
                term = inverse_ref[j] * total[f * 8 + j : f * 8 + j + 1, :]
                running = term if running is None else running + term
            head, rest = split(running)
            tail = (running - head.astype(jnp.float32) - rest.astype(jnp.float32)).astype(jnp.bfloat16)
            heads[f * 8 : f * 8 + 8] = head.astype(jnp.float32)
            rests[f * 8 : f * 8 + 8] = rest.astype(jnp.float32)
            tails[f * 8 : f * 8 + 8] = tail.astype(jnp.float32)

    hot = (lax.broadcasted_iota(jnp.int32, (cells, LANES), 0) == map_ref[...]).astype(jnp.bfloat16)
    spread = (
        mxu(heads[...].astype(jnp.bfloat16), hot)
        + mxu(rests[...].astype(jnp.bfloat16), hot)
        + mxu(tails[...].astype(jnp.bfloat16), hot)
    )
    ramp = prolong[:, 1]
    ramp_rows = column(list(ramp))
    for f in range(fields):
        quad = []
        for ab in range(4):
            at = f * 8 + 2 * ab
            down, up = spread[at : at + 1, :], spread[at + 1 : at + 2, :]
            quad.append(down + ramp_rows * (up - down))
        for j in range(nodes):
            down = quad[0] + float(ramp[j]) * (quad[1] - quad[0])
            slope = quad[2] + float(ramp[j]) * (quad[3] - quad[2]) - down
            for i in range(nodes):
                out_ref[f, i, j] = p_ref[f, i, j] + (down + float(ramp[i]) * slope)


def corrected_field(pressure, coarse_inverse, cell_row, sums, prolong):
    fields, nodes, elems = pressure.shape[0], pressure.shape[1], pressure.shape[-1]
    cells = coarse_inverse.shape[-1]
    field_spec = pl.BlockSpec((fields, nodes, nodes, nodes, LANES), lambda s: (0, 0, 0, 0, s))
    sum_spec = pl.BlockSpec((fields * 8, cells), lambda s: (0, 0))
    return pl.pallas_call(
        functools.partial(correct_kernel, prolong=prolong, parts=len(sums)),
        out_shape=jax.ShapeDtypeStruct(pressure.shape, jnp.float32),
        grid=(elems // LANES,),
        in_specs=[
            field_spec,
            pl.BlockSpec(coarse_inverse.shape, lambda s: (0, 0, 0)),
            pl.BlockSpec((1, LANES), lambda s: (0, s)),
        ]
        + [sum_spec] * len(sums),
        out_specs=field_spec,
        scratch_shapes=[pltpu.VMEM((fields * 8, cells), jnp.float32)] * 3,
        compiler_params=pltpu.CompilerParams(vmem_limit_bytes=16 * MIB),
        cost_estimate=pl.CostEstimate(flops=10**8, bytes_accessed=5 * 10**6, transcendentals=0),
        name="correct",
    )(pressure, coarse_inverse, cell_row, *sums)


def solution(mesh):
    blk_count, sub_count = mesh.shape["blk"], mesh.shape["sub"]

    def shifted(block, k):
        da, db = k // 3 - 1, k % 3 - 1
        pairs = []
        for b in range(blk_count):
            for u in range(sub_count):
                source = ((b + da) % blk_count) * sub_count + (u + db) % sub_count
                pairs.append((source, b * sub_count + u))
        size = block.shape[0] // 9
        return lax.ppermute(block[(8 - k) * size : (9 - k) * size], ("blk", "sub"), pairs)

    def on_device(
        pressure,
        right_side,
        geometry,
        face_weight,
        face_metric,
        cross_slots,
        local_pairs,
        coarse_map,
        coarse_inverse,
    ):
        fields, nodes, elems = pressure.shape[0], pressure.shape[1], pressure.shape[-1]
        derivative = derivative_matrix(nodes)
        points = node_points()
        prolong = np.stack([(1.0 - points) / 2.0, (1.0 + points) / 2.0], axis=1)
        cells = coarse_inverse.shape[-1]
        cell_row = coarse_map.reshape(1, elems)
        cross = cross_slots[1, 0] * elems + cross_slots[0, 0]
        pairs = jnp.concatenate(
            [local_pairs[1] * elems + local_pairs[0], local_pairs[3] * elems + local_pairs[2]]
        )
        width = fields + 1
        table, send = traces(
            cross * width,
            pltpu.with_memory_space_constraint(pressure, pltpu.HBM),
            pltpu.with_memory_space_constraint(jnp.transpose(face_weight, (1, 0, 2)), pltpu.HBM),
            pltpu.with_memory_space_constraint(jnp.transpose(face_metric, (1, 0, 2)), pltpu.HBM),
            derivative,
        )
        received = {k: shifted(send, k) for k in (3, 5, 1, 7)}
        local_rows = local_fluxes(pairs * width, pairs * fields, local_pairs, table, fields, nodes, elems)
        later, local_rows, right_later = lax.optimization_barrier((send, local_rows, right_side))
        received.update({k: shifted(later, k) for k in (0, 2, 6, 8)})
        start = volume(pressure, right_later, geometry, derivative)
        received = [received[k] for k in sorted(received)]
        residual, sums = residuals(
            cross * fields, cross_slots, send, received, start, local_rows, cell_row, cells, derivative, prolong
        )
        all_sums = [sums]
        for shift in range(1, sub_count):
            ring = [(at, (at + shift) % sub_count) for at in range(sub_count)]
            all_sums.append(lax.ppermute(sums, "sub", ring))
        return residual, corrected_field(pressure, coarse_inverse, cell_row, all_sums, prolong)

    split_elems = ("blk", "sub")
    field_spec = P(None, None, None, None, split_elems)

    return jax.shard_map(
        on_device,
        mesh=mesh,
        in_specs=(
            field_spec,
            field_spec,
            field_spec,
            P(None, None, split_elems),
            P(None, None, split_elems),
            P(None, split_elems, None),
            P(None, split_elems),
            P(split_elems),
            P(None, None, "blk"),
        ),
        out_specs=(field_spec, field_spec),
        check_vma=False,
    )
```

```python
import functools

import jax
import jax.numpy as jnp
import numpy as np
from jax import lax
from jax.experimental import pallas as pl
from jax.experimental.pallas import tpu as pltpu
from jax.sharding import PartitionSpec as P


LANES = 128
MIB = 1024 * 1024


def node_points():
    positive = [0.2092992179024789, 0.5917001814331423, 0.8717401485096066, 1.0]
    return np.array(sorted([-entry for entry in positive] + positive))


def derivative_matrix(node_count):
    points = node_points()
    weights = np.array(
        [
            1.0 / np.prod([points[row] - points[col] for col in range(node_count) if col != row])
            for row in range(node_count)
        ]
    )
    matrix = np.zeros((node_count, node_count))
    for row in range(node_count):
        for col in range(node_count):
            if row != col:
                matrix[row, col] = weights[col] / weights[row] / (points[row] - points[col])
        matrix[row, row] = -np.sum(matrix[row])
    return matrix


def inverse_code(code):
    swapped = 4 + 2 * jnp.bitwise_and(code, 1) + jnp.bitwise_and(jnp.right_shift(code, 1), 1)
    return jnp.where(code >= 4, swapped, code)


def spread_down(row):
    return jnp.broadcast_to(row, (LANES, LANES)).T


def lane_order(code, nodes):
    lane = lax.broadcasted_iota(jnp.int32, code.shape, 1)
    half = nodes * nodes
    place = jnp.bitwise_and(lane, half - 1)
    one, two = place // nodes, jnp.bitwise_and(place, nodes - 1)
    other = lane - place + two * nodes + one
    first = jnp.bitwise_and(code, 1) * ((nodes - 1) * nodes)
    second = jnp.bitwise_and(jnp.right_shift(code, 1), 1) * (nodes - 1)
    return jnp.bitwise_xor(jnp.where(jnp.bitwise_and(code, 4) > 0, other, lane), first + second)


def column(values):
    place = lax.broadcasted_iota(jnp.int32, (len(values), LANES), 0)
    result = jnp.full((len(values), LANES), float(values[0]), jnp.float32)
    for at, value in enumerate(values[1:], 1):
        result = jnp.where(place == at, float(value), result)
    return result


def weighted(factors, terms):
    running = None
    for factor, term in zip(factors, terms):
        if float(factor) == 0.0:
            continue
        product = term if float(factor) == 1.0 else float(factor) * term
        running = product if running is None else running + product
    return running


def derive(matrix, terms):
    count = len(terms)
    half = count // 2
    even = [terms[k] + terms[count - 1 - k] for k in range(half)]
    odd = [terms[k] - terms[count - 1 - k] for k in range(half)]
    low, high = [], []
    for i in range(half):
        plus = weighted([0.5 * (matrix[i, k] + matrix[i, count - 1 - k]) for k in range(half)], even)
        minus = weighted([0.5 * (matrix[i, k] - matrix[i, count - 1 - k]) for k in range(half)], odd)
        low.append(minus + plus)
        high.append(minus - plus)
    return low + high[::-1]


def split(value):
    head = value.astype(jnp.bfloat16)
    return head, (value - head.astype(jnp.float32)).astype(jnp.bfloat16)


def mxu(left, right, dims=(((1,), (0,)), ((), ()))):
    return lax.dot_general(left, right, dims, preferred_element_type=jnp.float32)


def trace_kernel(rows_ref, p_ref, fw_ref, fm_ref, table, send_ref, nat, *, derivative, elems):
    step = pl.program_id(0)
    steps = pl.num_programs(0)
    fields, nodes = p_ref.shape[0], p_ref.shape[1]
    pieces_total = fields + 1
    face_size = nodes * nodes
    last = nodes - 1
    flat = p_ref.reshape(fields * nodes * nodes * nodes, LANES)
    base = step * LANES
    low = [-derivative[0, k] for k in range(nodes)]
    high = [derivative[last, k] for k in range(nodes)]

    def put(face, piece, part):
        table[pl.ds((face * elems + base) * pieces_total + piece, LANES, stride=pieces_total), :] = part.T

    for face in range(6):
        put(face, fields, jnp.concatenate([fw_ref[face], fm_ref[face]], axis=0))

    for f in range(fields):
        for axis in range(3):
            for at in range(nodes):
                if axis == 0:
                    terms = [p_ref[f, k, at] for k in range(nodes)]
                elif axis == 1:
                    terms = [p_ref[f, at, k] for k in range(nodes)]
                else:
                    first = (f * nodes + at) * nodes * nodes
                    terms = [flat[pl.ds(first + k, nodes, stride=nodes), :] for k in range(nodes)]
                rows = slice(at * nodes, (at + 1) * nodes)
                more = slice(face_size + at * nodes, face_size + (at + 1) * nodes)
                nat[f, 2 * axis, rows] = terms[0]
                nat[f, 2 * axis, more] = weighted(low, terms)
                nat[f, 2 * axis + 1, rows] = terms[last]
                nat[f, 2 * axis + 1, more] = weighted(high, terms)
            put(2 * axis, f, nat[f, 2 * axis])
            put(2 * axis + 1, f, nat[f, 2 * axis + 1])

    @pl.when(step == steps - 1)
    def _():
        group_size = 16
        slot_total = send_ref.shape[0] // pieces_total

        def pick(group, carry):
            for u in range(group_size):
                k = group * group_size + u
                send_ref[pl.ds(k * pieces_total, pieces_total), :] = table[pl.ds(rows_ref[k], pieces_total), :]
            return carry

        lax.fori_loop(0, slot_total // group_size, pick, 0)


def traces(rows, pressure, face_weight, face_metric, derivative):
    fields, nodes, elems = pressure.shape[0], pressure.shape[1], pressure.shape[-1]
    face_size = nodes * nodes
    slot_total = rows.shape[0]
    face_spec = pl.BlockSpec((6, face_size, LANES), lambda s: (0, 0, s))
    whole = pl.BlockSpec(memory_space=pltpu.VMEM)
    return pl.pallas_call(
        functools.partial(trace_kernel, derivative=derivative, elems=elems),
        out_shape=(
            jax.ShapeDtypeStruct((6 * elems * (fields + 1), LANES), jnp.float32),
            jax.ShapeDtypeStruct((slot_total * (fields + 1), LANES), jnp.float32),
        ),
        grid=(elems // LANES,),
        in_specs=[
            pl.BlockSpec(memory_space=pltpu.SMEM),
            pl.BlockSpec((fields, nodes, nodes, nodes, LANES), lambda s: (0, 0, 0, 0, s)),
            face_spec,
            face_spec,
        ],
        out_specs=(whole, whole),
        scratch_shapes=[pltpu.VMEM((fields, 6, 2 * face_size, LANES), jnp.float32)],
        compiler_params=pltpu.CompilerParams(vmem_limit_bytes=6 * MIB),
        cost_estimate=pl.CostEstimate(flops=10**7, bytes_accessed=9 * 10**6, transcendentals=0),
        name="traces",
    )(rows, pressure, face_weight, face_metric)


def flux_rows(own, other, order, fields, nodes):
    half = nodes * nodes
    penalty = nodes * (nodes + 1) / 2.0
    lane = lax.broadcasted_iota(jnp.int32, order.shape, 1)
    head = lane < half
    turned = [jnp.take_along_axis(piece, order, axis=1) for piece in other]
    own_wm, other_wm = own[fields], turned[fields]
    mean = 0.5 * (own_wm + other_wm)
    swapped = pltpu.roll(mean, half, 1)
    weight = jnp.where(head, mean, swapped)
    own_scale = jnp.where(head, 1.0, own_wm)
    other_scale = jnp.where(head, 1.0, other_wm)
    direct = jnp.where(head, penalty * weight * swapped, 0.0)
    crossed = -0.5 * weight * own_scale
    results = []
    for f in range(fields):
        gap = own[f] * own_scale - turned[f] * other_scale
        results.append(direct * gap + crossed * pltpu.roll(gap, half, 1))
    return results


def pieces(ref, start, rows, fields):
    return [ref[pl.ds(start * (fields + 1) + f, rows, stride=fields + 1), :] for f in range(fields + 1)]


def cross_flags(slots_ref, flags):
    slot_total = slots_ref.shape[-1]
    code = jnp.where(slots_ref[3] > 0, slots_ref[4], inverse_code(slots_ref[4]))
    row = (code + 8 * slots_ref[2]).astype(jnp.float32)
    row = jnp.concatenate([row, jnp.zeros((1, flags.shape[0] - slot_total), jnp.float32)], axis=1)
    for at in range(flags.shape[0] // LANES):
        lanes = slice(at * LANES, (at + 1) * LANES)
        flags[lanes, :] = spread_down(row[:, lanes]).astype(jnp.int32)


def cross_rows(sources, own_ref, flags, result, cap, fields, nodes):
    rows = min(cap, 64)
    for k, (ref, place) in sources.items():
        for part in range(cap // rows):
            first = k * cap + part * rows
            flag = flags[first : first + rows, :]
            values = flux_rows(
                pieces(own_ref, first, rows, fields),
                pieces(ref, place * cap + part * rows, rows, fields),
                lane_order(flag, nodes),
                fields,
                nodes,
            )
            for f in range(fields):
                result[pl.ds(first * fields + f, rows, stride=fields), :] = jnp.where(flag >= 8, values[f], 0.0)


def put_blocks(blocks, to_ref, result, rows_ref, cap, fields):
    group_size = 16
    for k in blocks:

        def put(group, carry, k=k):
            for u in range(group_size):
                at = k * cap + group * group_size + u
                rows_ref[pl.ds(to_ref[at], fields), :] = result[pl.ds(at * fields, fields), :]
            return carry

        lax.fori_loop(0, cap // group_size, put, 0)


def three_parts(value):
    head, rest = split(value)
    return head, rest, (value - head.astype(jnp.float32) - rest.astype(jnp.float32)).astype(jnp.bfloat16)


def cell_mask(map_row, cells):
    place = lax.broadcasted_iota(jnp.int32, (cells, map_row.shape[1]), 0)
    return (place == map_row).astype(jnp.bfloat16)


def restrict_nodes(read, modes, at, ramp, nodes):
    ramp_rows = column(list(ramp))
    spots = [[None, None], [None, None]]
    for i in range(nodes):
        pencil = [read(i, j) for j in range(nodes)]
        for b, part in enumerate((weighted([1.0] * nodes, pencil), weighted(list(ramp), pencil))):
            spots[0][b] = part if i == 0 else spots[0][b] + part
            if float(ramp[i]) != 0.0:
                extra = float(ramp[i]) * part
                spots[1][b] = extra if spots[1][b] is None else spots[1][b] + extra
    for a in range(2):
        sides = [spots[1][b] if a == 1 else spots[0][b] - spots[1][b] for b in range(2)]
        for b, part in enumerate((sides[0] - sides[1], sides[1])):
            whole = jnp.sum(part, axis=0, keepdims=True)
            up = jnp.sum(part * ramp_rows, axis=0, keepdims=True)
            modes[at + 4 * a + 2 * b : at + 4 * a + 2 * b + 1, :] = whole - up
            modes[at + 4 * a + 2 * b + 1 : at + 4 * a + 2 * b + 2, :] = up


def face_modes(derivative, prolong):
    nodes = derivative.shape[0]
    ends = (0, nodes - 1)
    table = np.zeros((6, 2, nodes, nodes, 2, 2, 2))
    for axis in range(3):
        for side, end in enumerate(ends):
            slope = (-derivative[0] if side == 0 else derivative[end]) @ prolong
            for which, weights in enumerate((prolong[end], slope)):
                grid = np.einsum("x,py,qz->pqxyz", weights, prolong, prolong)
                table[2 * axis + side, which] = np.moveaxis(grid, 2, 2 + axis)
    return table.reshape(6, 2 * nodes * nodes, 8)


def local_kernel(from_ref, to_ref, code_ref, table_ref, out_ref, picked, order, result, *, fields, nodes):
    total = from_ref.shape[0]
    count = total // 2
    width = fields + 1
    group_size = 16
    out_ref[...] = jnp.zeros_like(out_ref)

    def pick(group, carry):
        for u in range(group_size):
            k = group * group_size + u
            picked[pl.ds(k * width, width), :] = table_ref[pl.ds(from_ref[k], width), :]
        return carry

    lax.fori_loop(0, total // group_size, pick, 0)
    for at in range(count // LANES):
        code = code_ref[4:5, at * LANES : (at + 1) * LANES]
        column_code = spread_down(code.astype(jnp.float32)).astype(jnp.int32)
        order[at * LANES : (at + 1) * LANES, :] = lane_order(column_code, nodes)
        order[count + at * LANES : count + (at + 1) * LANES, :] = lane_order(inverse_code(column_code), nodes)
    rows = min(count, 256)

    def flux(at, carry):
        start = at * rows
        other = lax.rem(start + count, total)
        values = flux_rows(
            pieces(picked, start, rows, fields),
            pieces(picked, other, rows, fields),
            order[pl.ds(pl.multiple_of(start, rows), rows), :],
            fields,
            nodes,
        )
        for f in range(fields):
            result[pl.ds(start * fields + f, rows, stride=fields), :] = values[f]
        return carry

    lax.fori_loop(0, total // rows, flux, 0)

    def place(group, carry):
        for u in range(group_size):
            k = group * group_size + u
            out_ref[pl.ds(to_ref[k], fields), :] = result[pl.ds(k * fields, fields), :]
        return carry

    lax.fori_loop(0, total // group_size, place, 0)


def local_fluxes(rows_from, rows_to, local_pairs, table, fields, nodes, elems):
    total = rows_from.shape[0]
    vmem = pl.BlockSpec(memory_space=pltpu.VMEM)
    smem = pl.BlockSpec(memory_space=pltpu.SMEM)
    return pl.pallas_call(
        functools.partial(local_kernel, fields=fields, nodes=nodes),
        out_shape=jax.ShapeDtypeStruct((6 * elems * fields, LANES), jnp.float32),
        in_specs=[smem, smem, vmem, vmem],
        out_specs=vmem,
        scratch_shapes=[
            pltpu.VMEM((total * (fields + 1), LANES), jnp.float32),
            pltpu.VMEM((total, LANES), jnp.int32),
            pltpu.VMEM((total * fields, LANES), jnp.float32),
        ],
        compiler_params=pltpu.CompilerParams(vmem_limit_bytes=8 * MIB),
        cost_estimate=pl.CostEstimate(flops=10**7, bytes_accessed=12 * 10**6, transcendentals=0),
        name="local_fluxes",
    )(rows_from, rows_to, local_pairs, table)


def volume_kernel(
    p_ref, rs_ref, g_ref, fwd_ref, back_ref, map_ref, *refs, derivative, ramp, earlier
):
    base_ref = refs[1] if earlier else None
    out_ref, sums_ref, one, two, three, four, modes = refs[2:] if earlier else refs
    fields, nodes = p_ref.shape[0], p_ref.shape[1]
    rows = nodes**3
    block = back_ref.shape[0]
    planes = block // (nodes * nodes)
    back = derivative.T

    def both(at, read):
        return jnp.concatenate([read(f).reshape(rows, LANES)[at * block : (at + 1) * block] for f in range(fields)], axis=1)

    for at in range(rows // block):
        head, tail = split(both(at, lambda f: p_ref[f]))
        slopes = mxu(fwd_ref[...], jnp.concatenate([head, tail, head], axis=0))
        for f in range(fields):
            lanes = slice(f * LANES, (f + 1) * LANES)
            here = slice(at * planes, (at + 1) * planes)
            two[f, here] = slopes[:block, lanes].reshape(planes, nodes, nodes, LANES)
            three[f, here] = slopes[block:, lanes].reshape(planes, nodes, nodes, LANES)
    for f in range(fields):
        for j in range(nodes):
            slopes = derive(derivative, [p_ref[f, k, j] for k in range(nodes)])
            for i in range(nodes):
                one[f, i, j] = slopes[i]
    for i in range(nodes):
        for j in range(nodes):
            xx, yy, zz, xy, xz, yz = [g_ref[c, i, j] for c in range(6)]
            for f in range(fields):
                s1, s2, s3 = one[f, i, j], two[f, i, j], three[f, i, j]
                one[f, i, j] = xx * s1 + xy * s2 + xz * s3
                two[f, i, j] = xy * s1 + yy * s2 + yz * s3
                three[f, i, j] = xz * s1 + yz * s2 + zz * s3
    for at in range(rows // block):
        head2, tail2 = split(both(at, lambda f: two[f]))
        head3, tail3 = split(both(at, lambda f: three[f]))
        sums = mxu(back_ref[...], jnp.concatenate([head2, tail2, head2, head3, tail3, head3], axis=0))
        for f in range(fields):
            lanes = slice(f * LANES, (f + 1) * LANES)
            here = slice(at * planes, (at + 1) * planes)
            four[f, here] = rs_ref[f, here] - sums[:, lanes].reshape(planes, nodes, nodes, LANES)
    for f in range(fields):
        for j in range(nodes):
            sums = derive(back, [one[f, k, j] for k in range(nodes)])
            for i in range(nodes):
                out_ref[f, i, j] = four[f, i, j] - sums[i]
        restrict_nodes(lambda i, j, f=f: out_ref[f, i, j], modes, f * 8, ramp, nodes)
    hot = cell_mask(map_ref[...], sums_ref.shape[1])
    across = (((1,), (1,)), ((), ()))
    head, rest, tail = three_parts(modes[...])
    total = mxu(head, hot, across) + mxu(rest, hot, across) + mxu(tail, hot, across)

    @pl.when(pl.program_id(0) == 0)
    def _():
        sums_ref[...] = base_ref[...] + total if earlier else total

    @pl.when(pl.program_id(0) > 0)
    def _():
        sums_ref[...] += total


def volume(pressure, right_side, geometry, cell_row, cells, derivative, ramp, first, steps, earlier=()):
    fields, nodes = pressure.shape[0], pressure.shape[1]
    block = 256
    planes = block // (nodes * nodes)
    eye = np.eye(nodes)
    middle = np.kron(np.eye(planes), np.kron(derivative, eye))
    minor = np.kron(np.eye(planes), np.kron(eye, derivative))

    def parts(matrix):
        whole = jnp.asarray(matrix, jnp.float32)
        head = whole.astype(jnp.bfloat16)
        return head, (whole - head.astype(jnp.float32)).astype(jnp.bfloat16)

    head, tail = parts(np.concatenate([middle, minor], axis=0))
    forward = jnp.concatenate([head, head, tail], axis=1)
    (head2, tail2), (head3, tail3) = parts(middle.T), parts(minor.T)
    backward = jnp.concatenate([head2, head2, tail2, head3, head3, tail3], axis=1)
    whole = (fields, nodes, nodes, nodes, LANES)
    field_spec = pl.BlockSpec(whole, lambda s: (0, 0, 0, 0, s + first))
    vmem = pl.BlockSpec(memory_space=pltpu.VMEM)
    return pl.pallas_call(
        functools.partial(volume_kernel, derivative=derivative, ramp=ramp, earlier=bool(earlier)),
        out_shape=(
            jax.ShapeDtypeStruct(pressure.shape, jnp.float32),
            jax.ShapeDtypeStruct((fields * 8, cells), jnp.float32),
        ),
        grid=(steps,),
        in_specs=[
            field_spec,
            field_spec,
            pl.BlockSpec((6, nodes, nodes, nodes, LANES), lambda s: (0, 0, 0, 0, s + first)),
            vmem,
            vmem,
            pl.BlockSpec((1, LANES), lambda s: (0, s + first)),
        ]
        + [pl.BlockSpec(memory_space=pl.ANY), vmem][: len(earlier)],
        out_specs=(field_spec, vmem),
        scratch_shapes=[pltpu.VMEM(whole, jnp.float32)] * 4 + [pltpu.VMEM((fields * 8, LANES), jnp.float32)],
        input_output_aliases={6: 0} if earlier else {},
        compiler_params=pltpu.CompilerParams(vmem_limit_bytes=14 * MIB),
        cost_estimate=pl.CostEstimate(flops=10**9, bytes_accessed=13 * 10**6, transcendentals=0),
    )(pressure, right_side, geometry, forward, backward, cell_row, *earlier)


def cross_kernel(
    to_ref, slots_ref, own_ref, far_up, far_down, up_ref, down_ref, right_ref, left_ref, rows_in, map_ref, base_ref,
    table_ref,
    rows_ref, sums_ref, order, result, packed, *, elems, fields, nodes,
):
    slot_total = to_ref.shape[0]
    cap = slot_total // 9
    del rows_in
    sources = {8: (far_up, 0), 6: (far_up, 1), 2: (far_down, 0), 0: (far_down, 1)}
    sources.update({1: (down_ref, 0), 3: (left_ref, 0), 5: (right_ref, 0), 7: (up_ref, 0)})
    cross_flags(slots_ref, order)
    cross_rows(sources, own_ref, order, result, cap, fields, nodes)
    put_blocks(sources, to_ref, result, rows_ref, cap, fields)
    cells = base_ref.shape[1]
    size = table_ref.shape[0] // 2
    block = min(elems, 256)
    for at in range(elems // block):
        parts = [
            split(rows_ref[pl.ds((face * elems + at * block) * fields + f, block, stride=fields), :])
            for f in range(fields)
            for face in range(6)
        ]
        heads = jnp.concatenate([head for head, _ in parts], axis=1)
        tails = jnp.concatenate([tail for _, tail in parts], axis=1)
        packed[at * block : (at + 1) * block, :] = (
            mxu(heads, table_ref[:size]) + mxu(tails, table_ref[:size]) + mxu(heads, table_ref[size:])
        )
    hot = cell_mask(map_ref[...], cells)
    head, rest, tail = three_parts(packed[...])
    total = mxu(hot, head) + mxu(hot, rest) + mxu(hot, tail)
    sums_ref[...] = base_ref[...] - total.T[: base_ref.shape[0]]


def cross_sums(rows_to, slots, own, far, local_rows, cell_row, base, derivative, prolong, nodes):
    elems = cell_row.shape[1]
    fields = base.shape[0] // 8
    slot_total = rows_to.shape[0]
    padded = -(-slot_total // LANES) * LANES
    table = face_modes(derivative, prolong).reshape(-1, 8)
    wide = np.zeros((fields, table.shape[0], LANES))
    for f in range(fields):
        wide[f, :, f * 8 : f * 8 + 8] = table
    wide = jnp.asarray(wide.reshape(-1, LANES), jnp.float32)
    head = wide.astype(jnp.bfloat16)
    both = jnp.concatenate([head, (wide - head.astype(jnp.float32)).astype(jnp.bfloat16)], axis=0)
    vmem = pl.BlockSpec(memory_space=pltpu.VMEM)
    return pl.pallas_call(
        functools.partial(cross_kernel, elems=elems, fields=fields, nodes=nodes),
        out_shape=(
            jax.ShapeDtypeStruct(local_rows.shape, jnp.float32),
            jax.ShapeDtypeStruct(base.shape, jnp.float32),
        ),
        in_specs=[pl.BlockSpec(memory_space=pltpu.SMEM)] + [vmem] * 12,
        out_specs=(vmem, vmem),
        scratch_shapes=[
            pltpu.VMEM((padded, LANES), jnp.int32),
            pltpu.VMEM((slot_total * fields, LANES), jnp.float32),
            pltpu.VMEM((elems, LANES), jnp.float32),
        ],
        input_output_aliases={9: 0},
        compiler_params=pltpu.CompilerParams(vmem_limit_bytes=8 * MIB),
        cost_estimate=pl.CostEstimate(flops=10**8, bytes_accessed=4 * 10**6, transcendentals=0),
        name="cross_sums",
    )(rows_to, slots, own, *far, local_rows, cell_row, base, both)


def lift_kernel(start_ref, rows_ref, *refs, derivative, elems, first):
    res_ref, nat = refs[-2:]
    fields, nodes = res_ref.shape[0], res_ref.shape[1]
    half = nodes * nodes
    last = nodes - 1
    base = (pl.program_id(0) + first) * LANES
    here = pl.ds(pl.multiple_of(base, LANES), LANES)
    for f in range(fields):
        for face in range(6):
            nat[f, face] = rows_ref[pl.ds((face * elems + base) * fields + f, LANES, stride=fields), :].T
    value_low = column([1.0] + [0.0] * last)
    value_high = column([0.0] * last + [1.0])
    lift_low = column(list(-derivative[0]))
    lift_high = column(list(derivative[last]))
    for f in range(fields):
        for i in range(nodes):
            for j in range(nodes):
                value = start_ref[f, i, j, :, here]
                at_j = slice(j * nodes, (j + 1) * nodes)
                at_i = slice(i * nodes, (i + 1) * nodes)
                low_j = slice(half + j * nodes, half + (j + 1) * nodes)
                low_i = slice(half + i * nodes, half + (i + 1) * nodes)
                if i == 0:
                    value = value - nat[f, 0, at_j]
                if i == last:
                    value = value - nat[f, 1, at_j]
                value = value + float(derivative[0, i]) * nat[f, 0, low_j]
                value = value - float(derivative[last, i]) * nat[f, 1, low_j]
                if j == 0:
                    value = value - nat[f, 2, at_i]
                if j == last:
                    value = value - nat[f, 3, at_i]
                value = value + float(derivative[0, j]) * nat[f, 2, low_i]
                value = value - float(derivative[last, j]) * nat[f, 3, low_i]
                node = i * nodes + j
                value = value - value_low * nat[f, 4, node : node + 1]
                value = value - lift_low * nat[f, 4, half + node : half + node + 1]
                value = value - value_high * nat[f, 5, node : node + 1]
                value = value - lift_high * nat[f, 5, half + node : half + node + 1]
                res_ref[f, i, j] = value


def lift(start, rows, derivative, first, steps, earlier=()):
    fields, nodes, elems = start.shape[0], start.shape[1], start.shape[-1]
    vmem = pl.BlockSpec(memory_space=pltpu.VMEM)
    return pl.pallas_call(
        functools.partial(lift_kernel, derivative=derivative, elems=elems, first=first),
        out_shape=jax.ShapeDtypeStruct(start.shape, jnp.float32),
        grid=(steps,),
        in_specs=[vmem, vmem] + [pl.BlockSpec(memory_space=pl.ANY)] * len(earlier),
        out_specs=pl.BlockSpec((fields, nodes, nodes, nodes, LANES), lambda s: (0, 0, 0, 0, s + first)),
        scratch_shapes=[pltpu.VMEM((fields, 6, LANES, LANES), jnp.float32)],
        input_output_aliases={2: 0} if earlier else {},
        compiler_params=pltpu.CompilerParams(vmem_limit_bytes=6 * MIB),
        cost_estimate=pl.CostEstimate(flops=10**8, bytes_accessed=9 * 10**6, transcendentals=0),
    )(start, rows, *earlier)


def correct_kernel(p_ref, inverse_ref, map_ref, *refs, prolong, parts):
    sum_refs = refs[:parts]
    out_ref, heads, rests, tails = refs[parts:]
    step = pl.program_id(0)
    fields, nodes = p_ref.shape[0], p_ref.shape[1]
    here = pl.ds(pl.multiple_of(step * LANES, LANES), LANES)
    cells = inverse_ref.shape[-1]

    @pl.when(step == 0)
    def _():
        total = sum_refs[0][...]
        for ref in sum_refs[1:]:
            total = total + ref[...]
        for f in range(fields):
            running = None
            for j in range(8):
                term = inverse_ref[j] * total[f * 8 + j : f * 8 + j + 1, :]
                running = term if running is None else running + term
            head, rest = split(running)
            tail = (running - head.astype(jnp.float32) - rest.astype(jnp.float32)).astype(jnp.bfloat16)
            heads[f * 8 : f * 8 + 8] = head.astype(jnp.float32)
            rests[f * 8 : f * 8 + 8] = rest.astype(jnp.float32)
            tails[f * 8 : f * 8 + 8] = tail.astype(jnp.float32)

    hot = (lax.broadcasted_iota(jnp.int32, (cells, LANES), 0) == map_ref[...]).astype(jnp.bfloat16)
    spread = (
        mxu(heads[...].astype(jnp.bfloat16), hot)
        + mxu(rests[...].astype(jnp.bfloat16), hot)
        + mxu(tails[...].astype(jnp.bfloat16), hot)
    )
    ramp = prolong[:, 1]
    ramp_rows = column(list(ramp))
    for f in range(fields):
        quad = []
        for ab in range(4):
            at = f * 8 + 2 * ab
            down, up = spread[at : at + 1, :], spread[at + 1 : at + 2, :]
            quad.append(down + ramp_rows * (up - down))
        for j in range(nodes):
            down = quad[0] + float(ramp[j]) * (quad[1] - quad[0])
            slope = quad[2] + float(ramp[j]) * (quad[3] - quad[2]) - down
            for i in range(nodes):
                out_ref[f, i, j] = p_ref[f, i, j, :, here] + (down + float(ramp[i]) * slope)


def corrected_field(pressure, coarse_inverse, cell_row, sums, prolong):
    fields, nodes, elems = pressure.shape[0], pressure.shape[1], pressure.shape[-1]
    cells = coarse_inverse.shape[-1]
    field_spec = pl.BlockSpec((fields, nodes, nodes, nodes, LANES), lambda s: (0, 0, 0, 0, s))
    sum_spec = pl.BlockSpec((fields * 8, cells), lambda s: (0, 0))
    return pl.pallas_call(
        functools.partial(correct_kernel, prolong=prolong, parts=len(sums)),
        out_shape=jax.ShapeDtypeStruct(pressure.shape, jnp.float32),
        grid=(elems // LANES,),
        in_specs=[
            pl.BlockSpec(memory_space=pltpu.VMEM),
            pl.BlockSpec(coarse_inverse.shape, lambda s: (0, 0, 0)),
            pl.BlockSpec((1, LANES), lambda s: (0, s)),
        ]
        + [sum_spec] * len(sums),
        out_specs=field_spec,
        scratch_shapes=[pltpu.VMEM((fields * 8, cells), jnp.float32)] * 3,
        compiler_params=pltpu.CompilerParams(vmem_limit_bytes=6 * MIB),
        cost_estimate=pl.CostEstimate(flops=10**8, bytes_accessed=5 * 10**6, transcendentals=0),
        name="correct",
    )(pressure, coarse_inverse, cell_row, *sums)


def solution(mesh):
    sub_count = mesh.shape["sub"]

    def ring(axis, step):
        count = mesh.shape[axis]
        return axis, [((at + step) % count, at) for at in range(count)]

    def swap(value, axis, step):
        return lax.ppermute(value, *ring(axis, step))

    def both_ways(to_next, to_last, axis, paired):
        count = mesh.shape[axis]
        if count % 2 or not paired:
            return swap(to_last, axis, 1), swap(to_next, axis, -1)
        even = lax.axis_index(axis) % 2 == 0
        one = lax.ppermute(jnp.where(even, to_next, to_last), axis, [(at, at ^ 1) for at in range(count)])
        pairs = [(at, (at + (1 if at % 2 else -1)) % count) for at in range(count)]
        two = lax.ppermute(jnp.where(even, to_last, to_next), axis, pairs)
        return jnp.where(even, one, two), jnp.where(even, two, one)

    def on_device(
        pressure,
        right_side,
        geometry,
        face_weight,
        face_metric,
        cross_slots,
        local_pairs,
        coarse_map,
        coarse_inverse,
    ):
        fields, nodes, elems = pressure.shape[0], pressure.shape[1], pressure.shape[-1]
        derivative = derivative_matrix(nodes)
        points = node_points()
        prolong = np.stack([(1.0 - points) / 2.0, (1.0 + points) / 2.0], axis=1)
        cells = coarse_inverse.shape[-1]
        cell_row = coarse_map.reshape(1, elems)
        cross = cross_slots[1, 0] * elems + cross_slots[0, 0]
        pairs = jnp.concatenate(
            [local_pairs[1] * elems + local_pairs[0], local_pairs[3] * elems + local_pairs[2]]
        )
        width = fields + 1
        table, send = traces(
            cross * width,
            pltpu.with_memory_space_constraint(pressure, pltpu.HBM),
            pltpu.with_memory_space_constraint(jnp.transpose(face_weight, (1, 0, 2)), pltpu.HBM),
            pltpu.with_memory_space_constraint(jnp.transpose(face_metric, (1, 0, 2)), pltpu.HBM),
            derivative,
        )
        size = send.shape[0] // 9
        block = [send[k * size : (k + 1) * size] for k in range(9)]
        right, left = both_ways(
            jnp.concatenate([block[2], block[8]]), jnp.concatenate([block[0], block[6]]), "sub", False
        )
        up, down = both_ways(block[7], block[1], "blk", True)
        hbm = [pltpu.with_memory_space_constraint(value, pltpu.HBM) for value in (pressure, right_side, geometry)]
        steps = elems // LANES
        far_up, far_down = both_ways(
            jnp.concatenate([right[size:], left[size:]]), jnp.concatenate([right[:size], left[:size]]), "blk", True
        )
        right, left = both_ways(block[5], block[3], "sub", False)
        local_rows = local_fluxes(pairs * width, pairs * fields, local_pairs, table, fields, nodes, elems)
        start, sums = volume(*hbm, cell_row, cells, derivative, prolong[:, 1], 0, steps)
        rows, sums = cross_sums(
            cross * fields,
            cross_slots,
            send,
            (far_up, far_down, up, down, right, left),
            local_rows,
            cell_row,
            sums,
            derivative,
            prolong,
            nodes,
        )
        if sub_count == 4 and steps > 1:
            other = lax.ppermute(sums, "sub", [(at, at ^ 1) for at in range(sub_count)])
            residual = lift(start, rows, derivative, 0, steps // 2)
            sums = sums + other
            other = lax.ppermute(sums, "sub", [(at, at ^ 2) for at in range(sub_count)])
            residual = lift(start, rows, derivative, steps // 2, steps - steps // 2, (residual,))
            all_sums = [sums, other]
        else:
            all_sums = [sums] + [swap(sums, "sub", step) for step in range(1, sub_count)]
            residual = lift(start, rows, derivative, 0, steps)
        return residual, corrected_field(pressure, coarse_inverse, cell_row, all_sums, prolong)

    split_elems = ("blk", "sub")
    field_spec = P(None, None, None, None, split_elems)

    return jax.shard_map(
        on_device,
        mesh=mesh,
        in_specs=(
            field_spec,
            field_spec,
            field_spec,
            P(None, None, split_elems),
            P(None, None, split_elems),
            P(None, split_elems, None),
            P(None, split_elems),
            P(split_elems),
            P(None, None, "blk"),
        ),
        out_specs=(field_spec, field_spec),
        check_vma=False,
    )
```

```python
import functools

import jax
import jax.numpy as jnp
import numpy as np
from jax import lax
from jax.experimental import pallas as pl
from jax.experimental.pallas import tpu as pltpu
from jax.sharding import PartitionSpec as P


LANES = 128
MIB = 1024 * 1024


def node_points():
    positive = [0.2092992179024789, 0.5917001814331423, 0.8717401485096066, 1.0]
    return np.array(sorted([-entry for entry in positive] + positive))


def derivative_matrix(node_count):
    points = node_points()
    weights = np.array(
        [
            1.0 / np.prod([points[row] - points[col] for col in range(node_count) if col != row])
            for row in range(node_count)
        ]
    )
    matrix = np.zeros((node_count, node_count))
    for row in range(node_count):
        for col in range(node_count):
            if row != col:
                matrix[row, col] = weights[col] / weights[row] / (points[row] - points[col])
        matrix[row, row] = -np.sum(matrix[row])
    return matrix


def inverse_code(code):
    swapped = 4 + 2 * jnp.bitwise_and(code, 1) + jnp.bitwise_and(jnp.right_shift(code, 1), 1)
    return jnp.where(code >= 4, swapped, code)


def spread_down(row):
    return jnp.broadcast_to(row, (LANES, LANES)).T


def lane_order(code, nodes):
    lane = lax.broadcasted_iota(jnp.int32, code.shape, 1)
    half = nodes * nodes
    place = jnp.bitwise_and(lane, half - 1)
    one, two = place // nodes, jnp.bitwise_and(place, nodes - 1)
    other = lane - place + two * nodes + one
    first = jnp.bitwise_and(code, 1) * ((nodes - 1) * nodes)
    second = jnp.bitwise_and(jnp.right_shift(code, 1), 1) * (nodes - 1)
    return jnp.bitwise_xor(jnp.where(jnp.bitwise_and(code, 4) > 0, other, lane), first + second)


def column(values):
    place = lax.broadcasted_iota(jnp.int32, (len(values), LANES), 0)
    result = jnp.full((len(values), LANES), float(values[0]), jnp.float32)
    for at, value in enumerate(values[1:], 1):
        result = jnp.where(place == at, float(value), result)
    return result


def weighted(factors, terms):
    running = None
    for factor, term in zip(factors, terms):
        if float(factor) == 0.0:
            continue
        product = term if float(factor) == 1.0 else float(factor) * term
        running = product if running is None else running + product
    return running


def derive(matrix, terms):
    count = len(terms)
    half = count // 2
    even = [terms[k] + terms[count - 1 - k] for k in range(half)]
    odd = [terms[k] - terms[count - 1 - k] for k in range(half)]
    low, high = [], []
    for i in range(half):
        plus = weighted([0.5 * (matrix[i, k] + matrix[i, count - 1 - k]) for k in range(half)], even)
        minus = weighted([0.5 * (matrix[i, k] - matrix[i, count - 1 - k]) for k in range(half)], odd)
        low.append(minus + plus)
        high.append(minus - plus)
    return low + high[::-1]


def split(value):
    head = value.astype(jnp.bfloat16)
    return head, (value - head.astype(jnp.float32)).astype(jnp.bfloat16)


def mxu(left, right, dims=(((1,), (0,)), ((), ()))):
    return lax.dot_general(left, right, dims, preferred_element_type=jnp.float32)


def trace_kernel(rows_ref, p_ref, fw_ref, fm_ref, table, send_ref, nat, *, derivative, elems):
    step = pl.program_id(0)
    steps = pl.num_programs(0)
    fields, nodes = p_ref.shape[0], p_ref.shape[1]
    pieces_total = fields + 1
    face_size = nodes * nodes
    last = nodes - 1
    flat = p_ref.reshape(fields * nodes * nodes * nodes, LANES)
    base = step * LANES
    low = [-derivative[0, k] for k in range(nodes)]
    high = [derivative[last, k] for k in range(nodes)]

    def put(face, piece, part):
        table[pl.ds((face * elems + base) * pieces_total + piece, LANES, stride=pieces_total), :] = part.T

    for face in range(6):
        put(face, fields, jnp.concatenate([fw_ref[face], fm_ref[face]], axis=0))

    for f in range(fields):
        for axis in range(3):
            for at in range(nodes):
                if axis == 0:
                    terms = [p_ref[f, k, at] for k in range(nodes)]
                elif axis == 1:
                    terms = [p_ref[f, at, k] for k in range(nodes)]
                else:
                    first = (f * nodes + at) * nodes * nodes
                    terms = [flat[pl.ds(first + k, nodes, stride=nodes), :] for k in range(nodes)]
                rows = slice(at * nodes, (at + 1) * nodes)
                more = slice(face_size + at * nodes, face_size + (at + 1) * nodes)
                nat[f, 2 * axis, rows] = terms[0]
                nat[f, 2 * axis, more] = weighted(low, terms)
                nat[f, 2 * axis + 1, rows] = terms[last]
                nat[f, 2 * axis + 1, more] = weighted(high, terms)
            put(2 * axis, f, nat[f, 2 * axis])
            put(2 * axis + 1, f, nat[f, 2 * axis + 1])

    @pl.when(step == steps - 1)
    def _():
        group_size = 16
        slot_total = send_ref.shape[0] // pieces_total

        def pick(group, carry):
            for u in range(group_size):
                k = group * group_size + u
                send_ref[pl.ds(k * pieces_total, pieces_total), :] = table[pl.ds(rows_ref[k], pieces_total), :]
            return carry

        lax.fori_loop(0, slot_total // group_size, pick, 0)


def traces(rows, pressure, face_weight, face_metric, derivative):
    fields, nodes, elems = pressure.shape[0], pressure.shape[1], pressure.shape[-1]
    face_size = nodes * nodes
    slot_total = rows.shape[0]
    face_spec = pl.BlockSpec((6, face_size, LANES), lambda s: (0, 0, s))
    whole = pl.BlockSpec(memory_space=pltpu.VMEM)
    return pl.pallas_call(
        functools.partial(trace_kernel, derivative=derivative, elems=elems),
        out_shape=(
            jax.ShapeDtypeStruct((6 * elems * (fields + 1), LANES), jnp.float32),
            jax.ShapeDtypeStruct((slot_total * (fields + 1), LANES), jnp.float32),
        ),
        grid=(elems // LANES,),
        in_specs=[
            pl.BlockSpec(memory_space=pltpu.SMEM),
            pl.BlockSpec((fields, nodes, nodes, nodes, LANES), lambda s: (0, 0, 0, 0, s)),
            face_spec,
            face_spec,
        ],
        out_specs=(whole, whole),
        scratch_shapes=[pltpu.VMEM((fields, 6, 2 * face_size, LANES), jnp.float32)],
        compiler_params=pltpu.CompilerParams(vmem_limit_bytes=6 * MIB),
        cost_estimate=pl.CostEstimate(flops=10**7, bytes_accessed=9 * 10**6, transcendentals=0),
        name="traces",
    )(rows, pressure, face_weight, face_metric)


def flux_rows(own, other, order, fields, nodes):
    half = nodes * nodes
    penalty = nodes * (nodes + 1) / 2.0
    lane = lax.broadcasted_iota(jnp.int32, order.shape, 1)
    head = lane < half
    turned = [jnp.take_along_axis(piece, order, axis=1) for piece in other]
    own_wm, other_wm = own[fields], turned[fields]
    mean = 0.5 * (own_wm + other_wm)
    swapped = pltpu.roll(mean, half, 1)
    weight = jnp.where(head, mean, swapped)
    own_scale = jnp.where(head, 1.0, own_wm)
    other_scale = jnp.where(head, 1.0, other_wm)
    direct = jnp.where(head, penalty * weight * swapped, 0.0)
    crossed = -0.5 * weight * own_scale
    results = []
    for f in range(fields):
        gap = own[f] * own_scale - turned[f] * other_scale
        results.append(direct * gap + crossed * pltpu.roll(gap, half, 1))
    return results


def pieces(ref, start, rows, fields):
    return [ref[pl.ds(start * (fields + 1) + f, rows, stride=fields + 1), :] for f in range(fields + 1)]


def cross_flags(slots_ref, flags):
    slot_total = slots_ref.shape[-1]
    code = jnp.where(slots_ref[3] > 0, slots_ref[4], inverse_code(slots_ref[4]))
    row = (code + 8 * slots_ref[2]).astype(jnp.float32)
    row = jnp.concatenate([row, jnp.zeros((1, flags.shape[0] - slot_total), jnp.float32)], axis=1)
    for at in range(flags.shape[0] // LANES):
        lanes = slice(at * LANES, (at + 1) * LANES)
        flags[lanes, :] = spread_down(row[:, lanes]).astype(jnp.int32)


def cross_rows(sources, own_ref, flags, result, cap, fields, nodes):
    rows = min(cap, 64)
    for k, (ref, place) in sources.items():
        for part in range(cap // rows):
            first = k * cap + part * rows
            flag = flags[first : first + rows, :]
            values = flux_rows(
                pieces(own_ref, first, rows, fields),
                pieces(ref, place * cap + part * rows, rows, fields),
                lane_order(flag, nodes),
                fields,
                nodes,
            )
            for f in range(fields):
                result[pl.ds(first * fields + f, rows, stride=fields), :] = jnp.where(flag >= 8, values[f], 0.0)


def put_blocks(blocks, to_ref, result, rows_ref, cap, fields):
    group_size = 16
    for k in blocks:

        def put(group, carry, k=k):
            for u in range(group_size):
                at = k * cap + group * group_size + u
                rows_ref[pl.ds(to_ref[at], fields), :] = result[pl.ds(at * fields, fields), :]
            return carry

        lax.fori_loop(0, cap // group_size, put, 0)


def three_parts(value):
    head, rest = split(value)
    return head, rest, (value - head.astype(jnp.float32) - rest.astype(jnp.float32)).astype(jnp.bfloat16)


def cell_mask(map_row, cells):
    place = lax.broadcasted_iota(jnp.int32, (cells, map_row.shape[1]), 0)
    return (place == map_row).astype(jnp.bfloat16)


def restrict_nodes(read, modes, at, ramp, nodes):
    ramp_rows = column(list(ramp))
    spots = [[None, None], [None, None]]
    for i in range(nodes):
        pencil = [read(i, j) for j in range(nodes)]
        for b, part in enumerate((weighted([1.0] * nodes, pencil), weighted(list(ramp), pencil))):
            spots[0][b] = part if i == 0 else spots[0][b] + part
            if float(ramp[i]) != 0.0:
                extra = float(ramp[i]) * part
                spots[1][b] = extra if spots[1][b] is None else spots[1][b] + extra
    for a in range(2):
        sides = [spots[1][b] if a == 1 else spots[0][b] - spots[1][b] for b in range(2)]
        for b, part in enumerate((sides[0] - sides[1], sides[1])):
            whole = jnp.sum(part, axis=0, keepdims=True)
            up = jnp.sum(part * ramp_rows, axis=0, keepdims=True)
            modes[at + 4 * a + 2 * b : at + 4 * a + 2 * b + 1, :] = whole - up
            modes[at + 4 * a + 2 * b + 1 : at + 4 * a + 2 * b + 2, :] = up


def face_modes(derivative, prolong):
    nodes = derivative.shape[0]
    ends = (0, nodes - 1)
    table = np.zeros((6, 2, nodes, nodes, 2, 2, 2))
    for axis in range(3):
        for side, end in enumerate(ends):
            slope = (-derivative[0] if side == 0 else derivative[end]) @ prolong
            for which, weights in enumerate((prolong[end], slope)):
                grid = np.einsum("x,py,qz->pqxyz", weights, prolong, prolong)
                table[2 * axis + side, which] = np.moveaxis(grid, 2, 2 + axis)
    return table.reshape(6, 2 * nodes * nodes, 8)


def local_kernel(from_ref, to_ref, code_ref, table_ref, out_ref, picked, order, result, *, fields, nodes):
    total = from_ref.shape[0]
    count = total // 2
    width = fields + 1
    group_size = 16
    out_ref[...] = jnp.zeros_like(out_ref)

    def pick(group, carry):
        for u in range(group_size):
            k = group * group_size + u
            picked[pl.ds(k * width, width), :] = table_ref[pl.ds(from_ref[k], width), :]
        return carry

    lax.fori_loop(0, total // group_size, pick, 0)
    for at in range(count // LANES):
        code = code_ref[4:5, at * LANES : (at + 1) * LANES]
        column_code = spread_down(code.astype(jnp.float32)).astype(jnp.int32)
        order[at * LANES : (at + 1) * LANES, :] = lane_order(column_code, nodes)
        order[count + at * LANES : count + (at + 1) * LANES, :] = lane_order(inverse_code(column_code), nodes)
    rows = min(count, 256)

    def flux(at, carry):
        start = at * rows
        other = lax.rem(start + count, total)
        values = flux_rows(
            pieces(picked, start, rows, fields),
            pieces(picked, other, rows, fields),
            order[pl.ds(pl.multiple_of(start, rows), rows), :],
            fields,
            nodes,
        )
        for f in range(fields):
            result[pl.ds(start * fields + f, rows, stride=fields), :] = values[f]
        return carry

    lax.fori_loop(0, total // rows, flux, 0)

    def place(group, carry):
        for u in range(group_size):
            k = group * group_size + u
            out_ref[pl.ds(to_ref[k], fields), :] = result[pl.ds(k * fields, fields), :]
        return carry

    lax.fori_loop(0, total // group_size, place, 0)


def local_fluxes(rows_from, rows_to, local_pairs, table, fields, nodes, elems):
    total = rows_from.shape[0]
    vmem = pl.BlockSpec(memory_space=pltpu.VMEM)
    smem = pl.BlockSpec(memory_space=pltpu.SMEM)
    return pl.pallas_call(
        functools.partial(local_kernel, fields=fields, nodes=nodes),
        out_shape=jax.ShapeDtypeStruct((6 * elems * fields, LANES), jnp.float32),
        in_specs=[smem, smem, vmem, vmem],
        out_specs=vmem,
        scratch_shapes=[
            pltpu.VMEM((total * (fields + 1), LANES), jnp.float32),
            pltpu.VMEM((total, LANES), jnp.int32),
            pltpu.VMEM((total * fields, LANES), jnp.float32),
        ],
        compiler_params=pltpu.CompilerParams(vmem_limit_bytes=8 * MIB),
        cost_estimate=pl.CostEstimate(flops=10**7, bytes_accessed=12 * 10**6, transcendentals=0),
        name="local_fluxes",
    )(rows_from, rows_to, local_pairs, table)


def volume_kernel(
    p_ref, rs_ref, g_ref, fwd_ref, back_ref, map_ref, out_ref, sums_ref, one, two, three, four, modes, *, derivative, ramp
):
    fields, nodes = p_ref.shape[0], p_ref.shape[1]
    rows = nodes**3
    block = back_ref.shape[0]
    planes = block // (nodes * nodes)
    back = derivative.T
    lanes_here = pl.ds(pl.multiple_of(pl.program_id(0) * LANES, LANES), LANES)

    def both(at, read):
        return jnp.concatenate([read(f).reshape(rows, LANES)[at * block : (at + 1) * block] for f in range(fields)], axis=1)

    for at in range(rows // block):
        head, tail = split(both(at, lambda f: p_ref[f, :, :, :, lanes_here]))
        slopes = mxu(fwd_ref[...], jnp.concatenate([head, tail, head], axis=0))
        for f in range(fields):
            lanes = slice(f * LANES, (f + 1) * LANES)
            here = slice(at * planes, (at + 1) * planes)
            two[f, here] = slopes[:block, lanes].reshape(planes, nodes, nodes, LANES)
            three[f, here] = slopes[block:, lanes].reshape(planes, nodes, nodes, LANES)
    for f in range(fields):
        for j in range(nodes):
            slopes = derive(derivative, [p_ref[f, k, j, :, lanes_here] for k in range(nodes)])
            for i in range(nodes):
                one[f, i, j] = slopes[i]
    for i in range(nodes):
        for j in range(nodes):
            xx, yy, zz, xy, xz, yz = [g_ref[c, i, j, :, lanes_here] for c in range(6)]
            for f in range(fields):
                s1, s2, s3 = one[f, i, j], two[f, i, j], three[f, i, j]
                one[f, i, j] = xx * s1 + xy * s2 + xz * s3
                two[f, i, j] = xy * s1 + yy * s2 + yz * s3
                three[f, i, j] = xz * s1 + yz * s2 + zz * s3
    for at in range(rows // block):
        head2, tail2 = split(both(at, lambda f: two[f]))
        head3, tail3 = split(both(at, lambda f: three[f]))
        sums = mxu(back_ref[...], jnp.concatenate([head2, tail2, head2, head3, tail3, head3], axis=0))
        for f in range(fields):
            lanes = slice(f * LANES, (f + 1) * LANES)
            here = slice(at * planes, (at + 1) * planes)
            four[f, here] = rs_ref[f, here, :, :, lanes_here] - sums[:, lanes].reshape(planes, nodes, nodes, LANES)
    for f in range(fields):
        for j in range(nodes):
            sums = derive(back, [one[f, k, j] for k in range(nodes)])
            for i in range(nodes):
                out_ref[f, i, j, :, lanes_here] = four[f, i, j] - sums[i]
        restrict_nodes(lambda i, j, f=f: out_ref[f, i, j, :, lanes_here], modes, f * 8, ramp, nodes)
    hot = cell_mask(map_ref[...], sums_ref.shape[1])
    across = (((1,), (1,)), ((), ()))
    head, rest, tail = three_parts(modes[...])
    total = mxu(head, hot, across) + mxu(rest, hot, across) + mxu(tail, hot, across)

    @pl.when(pl.program_id(0) == 0)
    def _():
        sums_ref[...] = total

    @pl.when(pl.program_id(0) > 0)
    def _():
        sums_ref[...] += total


def volume(pressure, right_side, geometry, cell_row, cells, derivative, ramp):
    fields, nodes, elems = pressure.shape[0], pressure.shape[1], pressure.shape[-1]
    block = 256
    planes = block // (nodes * nodes)
    eye = np.eye(nodes)
    middle = np.kron(np.eye(planes), np.kron(derivative, eye))
    minor = np.kron(np.eye(planes), np.kron(eye, derivative))

    def parts(matrix):
        whole = jnp.asarray(matrix, jnp.float32)
        head = whole.astype(jnp.bfloat16)
        return head, (whole - head.astype(jnp.float32)).astype(jnp.bfloat16)

    head, tail = parts(np.concatenate([middle, minor], axis=0))
    forward = jnp.concatenate([head, head, tail], axis=1)
    (head2, tail2), (head3, tail3) = parts(middle.T), parts(minor.T)
    backward = jnp.concatenate([head2, head2, tail2, head3, head3, tail3], axis=1)
    whole = (fields, nodes, nodes, nodes, LANES)
    vmem = pl.BlockSpec(memory_space=pltpu.VMEM)
    return pl.pallas_call(
        functools.partial(volume_kernel, derivative=derivative, ramp=ramp),
        out_shape=(
            jax.ShapeDtypeStruct(pressure.shape, jnp.float32),
            jax.ShapeDtypeStruct((fields * 8, cells), jnp.float32),
        ),
        grid=(elems // LANES,),
        in_specs=[vmem] * 5 + [pl.BlockSpec((1, LANES), lambda s: (0, s))],
        out_specs=(vmem, vmem),
        scratch_shapes=[pltpu.VMEM(whole, jnp.float32)] * 4 + [pltpu.VMEM((fields * 8, LANES), jnp.float32)],
        compiler_params=pltpu.CompilerParams(vmem_limit_bytes=14 * MIB),
        cost_estimate=pl.CostEstimate(flops=10**9, bytes_accessed=13 * 10**6, transcendentals=0),
    )(pressure, right_side, geometry, forward, backward, cell_row)


def center_kernel(
    to_ref, slots_ref, own_ref, up_ref, down_ref, right_ref, left_ref, rows_in, rows_ref, order, result, *, fields, nodes
):
    cap = to_ref.shape[0] // 9
    del rows_in
    sources = {1: (down_ref, 0), 3: (left_ref, 1), 5: (right_ref, 1), 7: (up_ref, 0)}
    cross_flags(slots_ref, order)
    cross_rows(sources, own_ref, order, result, cap, fields, nodes)
    put_blocks(sources, to_ref, result, rows_ref, cap, fields)


def center_rows(rows_to, slots, own, near, local_rows, fields, nodes):
    slot_total = rows_to.shape[0]
    padded = -(-slot_total // LANES) * LANES
    vmem = pl.BlockSpec(memory_space=pltpu.VMEM)
    return pl.pallas_call(
        functools.partial(center_kernel, fields=fields, nodes=nodes),
        out_shape=(
            jax.ShapeDtypeStruct(local_rows.shape, jnp.float32),
            jax.ShapeDtypeStruct((padded, LANES), jnp.int32),
        ),
        in_specs=[pl.BlockSpec(memory_space=pltpu.SMEM)] + [vmem] * 7,
        out_specs=(vmem, vmem),
        scratch_shapes=[pltpu.VMEM((slot_total * fields, LANES), jnp.float32)],
        input_output_aliases={7: 0},
        compiler_params=pltpu.CompilerParams(vmem_limit_bytes=8 * MIB),
        cost_estimate=pl.CostEstimate(flops=10**7, bytes_accessed=10**6, transcendentals=0),
        name="center_rows",
    )(rows_to, slots, own, *near, local_rows)


def cross_kernel(
    to_ref, order, own_ref, far_up, far_down, rows_in, map_ref, base_ref, table_ref,
    rows_ref, sums_ref, result, *, elems, fields, nodes,
):
    slot_total = to_ref.shape[0]
    cap = slot_total // 9
    del rows_in
    sources = {8: (far_up, 0), 6: (far_up, 1), 2: (far_down, 0), 0: (far_down, 1)}
    cross_rows(sources, own_ref, order, result, cap, fields, nodes)
    put_blocks(sources, to_ref, result, rows_ref, cap, fields)
    across = (((1,), (1,)), ((), ()))
    values = []
    for f in range(fields):
        parts = [split(rows_ref[pl.ds(face * elems * fields + f, elems, stride=fields), :]) for face in range(6)]
        by_head = mxu(table_ref[...], jnp.concatenate([head for head, _ in parts], axis=1), across)
        by_tail = mxu(table_ref[...], jnp.concatenate([tail for _, tail in parts], axis=1), across)
        values.append(by_head[:8] + by_head[8:] + by_tail[:8])
    hot = cell_mask(map_ref[...], base_ref.shape[1])
    head, rest, tail = three_parts(jnp.concatenate(values, axis=0))
    sums_ref[...] = base_ref[...] - (mxu(head, hot, across) + mxu(rest, hot, across) + mxu(tail, hot, across))


def cross_sums(rows_to, flags, own, far, local_rows, cell_row, base, derivative, prolong, nodes):
    elems = cell_row.shape[1]
    fields = base.shape[0] // 8
    slot_total = rows_to.shape[0]
    table = jnp.asarray(face_modes(derivative, prolong).reshape(-1, 8).T, jnp.float32)
    head = table.astype(jnp.bfloat16)
    both = jnp.concatenate([head, (table - head.astype(jnp.float32)).astype(jnp.bfloat16)], axis=0)
    vmem = pl.BlockSpec(memory_space=pltpu.VMEM)
    return pl.pallas_call(
        functools.partial(cross_kernel, elems=elems, fields=fields, nodes=nodes),
        out_shape=(
            jax.ShapeDtypeStruct(local_rows.shape, jnp.float32),
            jax.ShapeDtypeStruct(base.shape, jnp.float32),
        ),
        in_specs=[pl.BlockSpec(memory_space=pltpu.SMEM)] + [vmem] * 8,
        out_specs=(vmem, vmem),
        scratch_shapes=[pltpu.VMEM((slot_total * fields, LANES), jnp.float32)],
        input_output_aliases={5: 0},
        compiler_params=pltpu.CompilerParams(vmem_limit_bytes=12 * MIB),
        cost_estimate=pl.CostEstimate(flops=10**8, bytes_accessed=4 * 10**6, transcendentals=0),
        name="cross_sums",
    )(rows_to, flags, own, *far, local_rows, cell_row, base, both)


def lift_kernel(start_ref, rows_ref, *refs, derivative, elems, first):
    res_ref, nat = refs[-2:]
    fields, nodes = res_ref.shape[0], res_ref.shape[1]
    half = nodes * nodes
    last = nodes - 1
    base = (pl.program_id(0) + first) * LANES
    here = pl.ds(pl.multiple_of(base, LANES), LANES)
    for f in range(fields):
        for face in range(6):
            nat[f, face] = rows_ref[pl.ds((face * elems + base) * fields + f, LANES, stride=fields), :].T
    value_low = column([1.0] + [0.0] * last)
    value_high = column([0.0] * last + [1.0])
    lift_low = column(list(-derivative[0]))
    lift_high = column(list(derivative[last]))
    for f in range(fields):
        for i in range(nodes):
            for j in range(nodes):
                value = start_ref[f, i, j, :, here]
                at_j = slice(j * nodes, (j + 1) * nodes)
                at_i = slice(i * nodes, (i + 1) * nodes)
                low_j = slice(half + j * nodes, half + (j + 1) * nodes)
                low_i = slice(half + i * nodes, half + (i + 1) * nodes)
                if i == 0:
                    value = value - nat[f, 0, at_j]
                if i == last:
                    value = value - nat[f, 1, at_j]
                value = value + float(derivative[0, i]) * nat[f, 0, low_j]
                value = value - float(derivative[last, i]) * nat[f, 1, low_j]
                if j == 0:
                    value = value - nat[f, 2, at_i]
                if j == last:
                    value = value - nat[f, 3, at_i]
                value = value + float(derivative[0, j]) * nat[f, 2, low_i]
                value = value - float(derivative[last, j]) * nat[f, 3, low_i]
                node = i * nodes + j
                value = value - value_low * nat[f, 4, node : node + 1]
                value = value - lift_low * nat[f, 4, half + node : half + node + 1]
                value = value - value_high * nat[f, 5, node : node + 1]
                value = value - lift_high * nat[f, 5, half + node : half + node + 1]
                res_ref[f, i, j] = value


def lift(start, rows, derivative, first, steps, earlier=()):
    fields, nodes, elems = start.shape[0], start.shape[1], start.shape[-1]
    vmem = pl.BlockSpec(memory_space=pltpu.VMEM)
    return pl.pallas_call(
        functools.partial(lift_kernel, derivative=derivative, elems=elems, first=first),
        out_shape=jax.ShapeDtypeStruct(start.shape, jnp.float32),
        grid=(steps,),
        in_specs=[vmem, vmem] + [pl.BlockSpec(memory_space=pl.ANY)] * len(earlier),
        out_specs=pl.BlockSpec((fields, nodes, nodes, nodes, LANES), lambda s: (0, 0, 0, 0, s + first)),
        scratch_shapes=[pltpu.VMEM((fields, 6, LANES, LANES), jnp.float32)],
        input_output_aliases={2: 0} if earlier else {},
        compiler_params=pltpu.CompilerParams(vmem_limit_bytes=6 * MIB),
        cost_estimate=pl.CostEstimate(flops=10**8, bytes_accessed=9 * 10**6, transcendentals=0),
    )(start, rows, *earlier)


def send_out(buffer, out_hbm, sems, step, f):
    cuts = sems.shape[2]
    size = buffer.shape[2] // cuts
    lanes = pl.ds(step * LANES if isinstance(step, int) else pl.multiple_of(step * LANES, LANES), LANES)
    return [
        pltpu.make_async_copy(
            buffer.at[step, f, cut * size : (cut + 1) * size],
            out_hbm.at[f, cut * size : (cut + 1) * size, :, :, lanes],
            sems.at[step, f, cut],
        )
        for cut in range(cuts)
    ]


def correct_kernel(p_ref, inverse_ref, map_ref, *refs, prolong, parts):
    sum_refs = refs[:parts]
    out_hbm, heads, rests, tails, buffer, sems = refs[parts:]
    step = pl.program_id(0)
    fields, nodes = p_ref.shape[0], p_ref.shape[1]
    here = pl.ds(pl.multiple_of(step * LANES, LANES), LANES)
    cells = inverse_ref.shape[-1]

    @pl.when(step == 0)
    def _():
        total = sum_refs[0][...]
        for ref in sum_refs[1:]:
            total = total + ref[...]
        for f in range(fields):
            running = None
            for j in range(8):
                term = inverse_ref[j] * total[f * 8 + j : f * 8 + j + 1, :]
                running = term if running is None else running + term
            head, rest = split(running)
            tail = (running - head.astype(jnp.float32) - rest.astype(jnp.float32)).astype(jnp.bfloat16)
            heads[f * 8 : f * 8 + 8] = head.astype(jnp.float32)
            rests[f * 8 : f * 8 + 8] = rest.astype(jnp.float32)
            tails[f * 8 : f * 8 + 8] = tail.astype(jnp.float32)

    hot = (lax.broadcasted_iota(jnp.int32, (cells, LANES), 0) == map_ref[...]).astype(jnp.bfloat16)
    spread = (
        mxu(heads[...].astype(jnp.bfloat16), hot)
        + mxu(rests[...].astype(jnp.bfloat16), hot)
        + mxu(tails[...].astype(jnp.bfloat16), hot)
    )
    ramp = prolong[:, 1]
    ramp_rows = column(list(ramp))
    for f in range(fields):
        quad = []
        for ab in range(4):
            at = f * 8 + 2 * ab
            down, up = spread[at : at + 1, :], spread[at + 1 : at + 2, :]
            quad.append(down + ramp_rows * (up - down))
        for j in range(nodes):
            down = quad[0] + float(ramp[j]) * (quad[1] - quad[0])
            slope = quad[2] + float(ramp[j]) * (quad[3] - quad[2]) - down
            for i in range(nodes):
                buffer[step, f, i, j] = p_ref[f, i, j, :, here] + (down + float(ramp[i]) * slope)
        for copy in send_out(buffer, out_hbm, sems, step, f):
            copy.start()

    @pl.when(step == pl.num_programs(0) - 1)
    def _():
        for at in range(buffer.shape[0]):
            for f in range(fields):
                for copy in send_out(buffer, out_hbm, sems, at, f):
                    copy.wait()


def corrected_field(pressure, coarse_inverse, cell_row, sums, prolong):
    fields, nodes, elems = pressure.shape[0], pressure.shape[1], pressure.shape[-1]
    cells = coarse_inverse.shape[-1]
    sum_spec = pl.BlockSpec((fields * 8, cells), lambda s: (0, 0))
    return pl.pallas_call(
        functools.partial(correct_kernel, prolong=prolong, parts=len(sums)),
        out_shape=jax.ShapeDtypeStruct(pressure.shape, jnp.float32),
        grid=(elems // LANES,),
        in_specs=[
            pl.BlockSpec(memory_space=pltpu.VMEM),
            pl.BlockSpec(coarse_inverse.shape, lambda s: (0, 0, 0)),
            pl.BlockSpec((1, LANES), lambda s: (0, s)),
        ]
        + [sum_spec] * len(sums),
        out_specs=pl.BlockSpec(memory_space=pl.ANY),
        scratch_shapes=[pltpu.VMEM((fields * 8, cells), jnp.float32)] * 3
        + [
            pltpu.VMEM((elems // LANES, fields, nodes, nodes, nodes, LANES), jnp.float32),
            pltpu.SemaphoreType.DMA((elems // LANES, fields, 4)),
        ],
        compiler_params=pltpu.CompilerParams(vmem_limit_bytes=6 * MIB),
        cost_estimate=pl.CostEstimate(flops=10**8, bytes_accessed=5 * 10**6, transcendentals=0),
        name="correct",
    )(pressure, coarse_inverse, cell_row, *sums)


def solution(mesh):
    sub_count = mesh.shape["sub"]

    def ring(axis, step):
        count = mesh.shape[axis]
        return axis, [((at + step) % count, at) for at in range(count)]

    def swap(value, axis, step):
        return lax.ppermute(value, *ring(axis, step))

    def both_ways(to_next, to_last, axis, paired):
        count = mesh.shape[axis]
        if count % 2 or not paired:
            return swap(to_last, axis, 1), swap(to_next, axis, -1)
        even = lax.axis_index(axis) % 2 == 0
        one = lax.ppermute(jnp.where(even, to_next, to_last), axis, [(at, at ^ 1) for at in range(count)])
        pairs = [(at, (at + (1 if at % 2 else -1)) % count) for at in range(count)]
        two = lax.ppermute(jnp.where(even, to_last, to_next), axis, pairs)
        return jnp.where(even, one, two), jnp.where(even, two, one)

    def on_device(
        pressure,
        right_side,
        geometry,
        face_weight,
        face_metric,
        cross_slots,
        local_pairs,
        coarse_map,
        coarse_inverse,
    ):
        fields, nodes, elems = pressure.shape[0], pressure.shape[1], pressure.shape[-1]
        derivative = derivative_matrix(nodes)
        points = node_points()
        prolong = np.stack([(1.0 - points) / 2.0, (1.0 + points) / 2.0], axis=1)
        cells = coarse_inverse.shape[-1]
        cell_row = coarse_map.reshape(1, elems)
        cross = cross_slots[1, 0] * elems + cross_slots[0, 0]
        pairs = jnp.concatenate(
            [local_pairs[1] * elems + local_pairs[0], local_pairs[3] * elems + local_pairs[2]]
        )
        width = fields + 1
        table, send = traces(
            cross * width,
            pltpu.with_memory_space_constraint(pressure, pltpu.HBM),
            pltpu.with_memory_space_constraint(jnp.transpose(face_weight, (1, 0, 2)), pltpu.HBM),
            pltpu.with_memory_space_constraint(jnp.transpose(face_metric, (1, 0, 2)), pltpu.HBM),
            derivative,
        )
        size = send.shape[0] // 9
        block = [send[k * size : (k + 1) * size] for k in range(9)]
        right, left = both_ways(
            jnp.concatenate([block[2], block[5], block[8]]),
            jnp.concatenate([block[0], block[3], block[6]]),
            "sub",
            False,
        )
        up, down = both_ways(block[7], block[1], "blk", True)
        steps = elems // LANES
        far_up, far_down = both_ways(
            jnp.concatenate([right[2 * size :], left[2 * size :]]),
            jnp.concatenate([right[:size], left[:size]]),
            "blk",
            True,
        )
        local_rows = local_fluxes(pairs * width, pairs * fields, local_pairs, table, fields, nodes, elems)
        start, sums = volume(pressure, right_side, geometry, cell_row, cells, derivative, prolong[:, 1])
        local_rows, flags = center_rows(
            cross * fields, cross_slots, send, (up, down, right, left), local_rows, fields, nodes
        )
        rows, sums = cross_sums(
            cross * fields,
            flags,
            send,
            (far_up, far_down),
            local_rows,
            cell_row,
            sums,
            derivative,
            prolong,
            nodes,
        )
        if sub_count == 4 and steps > 1:
            other = lax.ppermute(sums, "sub", [(at, at ^ 1) for at in range(sub_count)])
            residual = lift(start, rows, derivative, 0, steps // 2)
            sums = sums + other
            other = lax.ppermute(sums, "sub", [(at, at ^ 2) for at in range(sub_count)])
            residual = lift(start, rows, derivative, steps // 2, steps - steps // 2, (residual,))
            all_sums = [sums, other]
        else:
            all_sums = [sums] + [swap(sums, "sub", step) for step in range(1, sub_count)]
            residual = lift(start, rows, derivative, 0, steps)
        return residual, corrected_field(pressure, coarse_inverse, cell_row, all_sums, prolong)

    split_elems = ("blk", "sub")
    field_spec = P(None, None, None, None, split_elems)

    return jax.shard_map(
        on_device,
        mesh=mesh,
        in_specs=(
            field_spec,
            field_spec,
            field_spec,
            P(None, None, split_elems),
            P(None, None, split_elems),
            P(None, split_elems, None),
            P(None, split_elems),
            P(split_elems),
            P(None, None, "blk"),
        ),
        out_specs=(field_spec, field_spec),
        check_vma=False,
    )
```

```python
import functools

import jax
import jax.numpy as jnp
import numpy as np
from jax import lax
from jax.experimental import pallas as pl
from jax.experimental.pallas import tpu as pltpu
from jax.sharding import PartitionSpec as P


LANES = 128
MIB = 1024 * 1024


def node_points():
    positive = [0.2092992179024789, 0.5917001814331423, 0.8717401485096066, 1.0]
    return np.array(sorted([-entry for entry in positive] + positive))


def derivative_matrix(node_count):
    points = node_points()
    weights = np.array(
        [
            1.0 / np.prod([points[row] - points[col] for col in range(node_count) if col != row])
            for row in range(node_count)
        ]
    )
    matrix = np.zeros((node_count, node_count))
    for row in range(node_count):
        for col in range(node_count):
            if row != col:
                matrix[row, col] = weights[col] / weights[row] / (points[row] - points[col])
        matrix[row, row] = -np.sum(matrix[row])
    return matrix


def inverse_code(code):
    swapped = 4 + 2 * jnp.bitwise_and(code, 1) + jnp.bitwise_and(jnp.right_shift(code, 1), 1)
    return jnp.where(code >= 4, swapped, code)


def spread_down(row):
    return jnp.broadcast_to(row, (LANES, LANES)).T


def lane_order(code, nodes):
    lane = lax.broadcasted_iota(jnp.int32, code.shape, 1)
    half = nodes * nodes
    place = jnp.bitwise_and(lane, half - 1)
    one, two = place // nodes, jnp.bitwise_and(place, nodes - 1)
    other = lane - place + two * nodes + one
    first = jnp.bitwise_and(code, 1) * ((nodes - 1) * nodes)
    second = jnp.bitwise_and(jnp.right_shift(code, 1), 1) * (nodes - 1)
    return jnp.bitwise_xor(jnp.where(jnp.bitwise_and(code, 4) > 0, other, lane), first + second)


def column(values):
    place = lax.broadcasted_iota(jnp.int32, (len(values), LANES), 0)
    result = jnp.full((len(values), LANES), float(values[0]), jnp.float32)
    for at, value in enumerate(values[1:], 1):
        result = jnp.where(place == at, float(value), result)
    return result


def weighted(factors, terms):
    running = None
    for factor, term in zip(factors, terms):
        if float(factor) == 0.0:
            continue
        product = term if float(factor) == 1.0 else float(factor) * term
        running = product if running is None else running + product
    return running


def derive(matrix, terms):
    count = len(terms)
    half = count // 2
    even = [terms[k] + terms[count - 1 - k] for k in range(half)]
    odd = [terms[k] - terms[count - 1 - k] for k in range(half)]
    low, high = [], []
    for i in range(half):
        plus = weighted([0.5 * (matrix[i, k] + matrix[i, count - 1 - k]) for k in range(half)], even)
        minus = weighted([0.5 * (matrix[i, k] - matrix[i, count - 1 - k]) for k in range(half)], odd)
        low.append(minus + plus)
        high.append(minus - plus)
    return low + high[::-1]


def split(value):
    head = value.astype(jnp.bfloat16)
    return head, (value - head.astype(jnp.float32)).astype(jnp.bfloat16)


def mxu(left, right, dims=(((1,), (0,)), ((), ()))):
    return lax.dot_general(left, right, dims, preferred_element_type=jnp.float32)


def trace_kernel(rows_ref, *refs, derivative, elems):
    p_refs, (fw_ref, fm_ref, table, send_ref, nat) = refs[:-5], refs[-5:]
    step = pl.program_id(0)
    steps = pl.num_programs(0)
    fields, nodes = len(p_refs), p_refs[0].shape[1]
    pieces_total = fields + 1
    face_size = nodes * nodes
    last = nodes - 1
    flats = [ref.reshape(nodes * nodes * nodes, LANES) for ref in p_refs]
    base = step * LANES
    low = [-derivative[0, k] for k in range(nodes)]
    high = [derivative[last, k] for k in range(nodes)]

    def put(face, piece, part):
        table[pl.ds((face * elems + base) * pieces_total + piece, LANES, stride=pieces_total), :] = part.T

    for face in range(6):
        put(face, fields, jnp.concatenate([fw_ref[face], fm_ref[face]], axis=0))

    for f in range(fields):
        for axis in range(3):
            for at in range(nodes):
                if axis == 0:
                    terms = [p_refs[f][0, k, at] for k in range(nodes)]
                elif axis == 1:
                    terms = [p_refs[f][0, at, k] for k in range(nodes)]
                else:
                    first = at * nodes * nodes
                    terms = [flats[f][pl.ds(first + k, nodes, stride=nodes), :] for k in range(nodes)]
                rows = slice(at * nodes, (at + 1) * nodes)
                more = slice(face_size + at * nodes, face_size + (at + 1) * nodes)
                nat[f, 2 * axis, rows] = terms[0]
                nat[f, 2 * axis, more] = weighted(low, terms)
                nat[f, 2 * axis + 1, rows] = terms[last]
                nat[f, 2 * axis + 1, more] = weighted(high, terms)
            put(2 * axis, f, nat[f, 2 * axis])
            put(2 * axis + 1, f, nat[f, 2 * axis + 1])

    @pl.when(step == steps - 1)
    def _():
        group_size = 16
        slot_total = send_ref.shape[0] // pieces_total

        def pick(group, carry):
            for u in range(group_size):
                k = group * group_size + u
                send_ref[pl.ds(k * pieces_total, pieces_total), :] = table[pl.ds(rows_ref[k], pieces_total), :]
            return carry

        lax.fori_loop(0, slot_total // group_size, pick, 0)


def traces(rows, pressure, face_weight, face_metric, derivative):
    fields, nodes, elems = pressure.shape[0], pressure.shape[1], pressure.shape[-1]
    face_size = nodes * nodes
    slot_total = rows.shape[0]
    face_spec = pl.BlockSpec((6, face_size, LANES), lambda s: (0, 0, s))
    whole = pl.BlockSpec(memory_space=pltpu.VMEM)
    return pl.pallas_call(
        functools.partial(trace_kernel, derivative=derivative, elems=elems),
        out_shape=(
            jax.ShapeDtypeStruct((6 * elems * (fields + 1), LANES), jnp.float32),
            jax.ShapeDtypeStruct((slot_total * (fields + 1), LANES), jnp.float32),
        ),
        grid=(elems // LANES,),
        in_specs=[
            pl.BlockSpec(memory_space=pltpu.SMEM),
        ]
        + [
            pl.BlockSpec((1, nodes, nodes, nodes, LANES), lambda s, f=f: (f, 0, 0, 0, s)) for f in range(fields)
        ]
        + [face_spec, face_spec],
        out_specs=(whole, whole),
        scratch_shapes=[pltpu.VMEM((fields, 6, 2 * face_size, LANES), jnp.float32)],
        compiler_params=pltpu.CompilerParams(vmem_limit_bytes=6 * MIB),
        cost_estimate=pl.CostEstimate(flops=10**7, bytes_accessed=9 * 10**6, transcendentals=0),
        name="traces",
    )(rows, *[pressure] * fields, face_weight, face_metric)


def flux_rows(own, other, order, fields, nodes):
    half = nodes * nodes
    penalty = nodes * (nodes + 1) / 2.0
    lane = lax.broadcasted_iota(jnp.int32, order.shape, 1)
    head = lane < half
    turned = [jnp.take_along_axis(piece, order, axis=1) for piece in other]
    own_wm, other_wm = own[fields], turned[fields]
    mean = 0.5 * (own_wm + other_wm)
    swapped = pltpu.roll(mean, half, 1)
    weight = jnp.where(head, mean, swapped)
    own_scale = jnp.where(head, 1.0, own_wm)
    other_scale = jnp.where(head, 1.0, other_wm)
    direct = jnp.where(head, penalty * weight * swapped, 0.0)
    crossed = -0.5 * weight * own_scale
    results = []
    for f in range(fields):
        gap = own[f] * own_scale - turned[f] * other_scale
        results.append(direct * gap + crossed * pltpu.roll(gap, half, 1))
    return results


def pieces(ref, start, rows, fields):
    return [ref[pl.ds(start * (fields + 1) + f, rows, stride=fields + 1), :] for f in range(fields + 1)]


def cross_flags(slots_ref, flags):
    slot_total = slots_ref.shape[-1]
    code = jnp.where(slots_ref[3] > 0, slots_ref[4], inverse_code(slots_ref[4]))
    row = (code + 8 * slots_ref[2]).astype(jnp.float32)
    row = jnp.concatenate([row, jnp.zeros((1, flags.shape[0] - slot_total), jnp.float32)], axis=1)
    for at in range(flags.shape[0] // LANES):
        lanes = slice(at * LANES, (at + 1) * LANES)
        flags[lanes, :] = spread_down(row[:, lanes]).astype(jnp.int32)


def cross_rows(sources, own_ref, flags, result, cap, fields, nodes):
    rows = min(cap, 64)
    for k, (ref, place) in sources.items():
        for part in range(cap // rows):
            first = k * cap + part * rows
            flag = flags[first : first + rows, :]
            values = flux_rows(
                pieces(own_ref, first, rows, fields),
                pieces(ref, place * cap + part * rows, rows, fields),
                lane_order(flag, nodes),
                fields,
                nodes,
            )
            for f in range(fields):
                result[pl.ds(first * fields + f, rows, stride=fields), :] = jnp.where(flag >= 8, values[f], 0.0)


def put_blocks(blocks, to_ref, result, rows_ref, cap, fields):
    group_size = 16
    for k in blocks:

        def put(group, carry, k=k):
            for u in range(group_size):
                at = k * cap + group * group_size + u
                rows_ref[pl.ds(to_ref[at], fields), :] = result[pl.ds(at * fields, fields), :]
            return carry

        lax.fori_loop(0, cap // group_size, put, 0)


def three_parts(value):
    head, rest = split(value)
    return head, rest, (value - head.astype(jnp.float32) - rest.astype(jnp.float32)).astype(jnp.bfloat16)


def cell_mask(map_row, cells):
    place = lax.broadcasted_iota(jnp.int32, (cells, map_row.shape[1]), 0)
    return (place == map_row).astype(jnp.bfloat16)


def restrict_nodes(read, modes, at, ramp, nodes):
    ramp_rows = column(list(ramp))
    spots = [[None, None], [None, None]]
    for i in range(nodes):
        pencil = [read(i, j) for j in range(nodes)]
        for b, part in enumerate((weighted([1.0] * nodes, pencil), weighted(list(ramp), pencil))):
            spots[0][b] = part if i == 0 else spots[0][b] + part
            if float(ramp[i]) != 0.0:
                extra = float(ramp[i]) * part
                spots[1][b] = extra if spots[1][b] is None else spots[1][b] + extra
    for a in range(2):
        sides = [spots[1][b] if a == 1 else spots[0][b] - spots[1][b] for b in range(2)]
        for b, part in enumerate((sides[0] - sides[1], sides[1])):
            whole = jnp.sum(part, axis=0, keepdims=True)
            up = jnp.sum(part * ramp_rows, axis=0, keepdims=True)
            modes[at + 4 * a + 2 * b : at + 4 * a + 2 * b + 1, :] = whole - up
            modes[at + 4 * a + 2 * b + 1 : at + 4 * a + 2 * b + 2, :] = up


def face_modes(derivative, prolong):
    nodes = derivative.shape[0]
    ends = (0, nodes - 1)
    table = np.zeros((6, 2, nodes, nodes, 2, 2, 2))
    for axis in range(3):
        for side, end in enumerate(ends):
            slope = (-derivative[0] if side == 0 else derivative[end]) @ prolong
            for which, weights in enumerate((prolong[end], slope)):
                grid = np.einsum("x,py,qz->pqxyz", weights, prolong, prolong)
                table[2 * axis + side, which] = np.moveaxis(grid, 2, 2 + axis)
    return table.reshape(6, 2 * nodes * nodes, 8)


def local_kernel(from_ref, to_ref, code_ref, table_ref, out_ref, picked, order, result, *, fields, nodes):
    total = from_ref.shape[0]
    count = total // 2
    width = fields + 1
    group_size = 16
    out_ref[...] = jnp.zeros_like(out_ref)

    def pick(group, carry):
        for u in range(group_size):
            k = group * group_size + u
            picked[pl.ds(k * width, width), :] = table_ref[pl.ds(from_ref[k], width), :]
        return carry

    lax.fori_loop(0, total // group_size, pick, 0)
    for at in range(count // LANES):
        code = code_ref[4:5, at * LANES : (at + 1) * LANES]
        column_code = spread_down(code.astype(jnp.float32)).astype(jnp.int32)
        order[at * LANES : (at + 1) * LANES, :] = lane_order(column_code, nodes)
        order[count + at * LANES : count + (at + 1) * LANES, :] = lane_order(inverse_code(column_code), nodes)
    rows = min(count, 256)

    def flux(at, carry):
        start = at * rows
        other = lax.rem(start + count, total)
        values = flux_rows(
            pieces(picked, start, rows, fields),
            pieces(picked, other, rows, fields),
            order[pl.ds(pl.multiple_of(start, rows), rows), :],
            fields,
            nodes,
        )
        for f in range(fields):
            result[pl.ds(start * fields + f, rows, stride=fields), :] = values[f]
        return carry

    lax.fori_loop(0, total // rows, flux, 0)

    def place(group, carry):
        for u in range(group_size):
            k = group * group_size + u
            out_ref[pl.ds(to_ref[k], fields), :] = result[pl.ds(k * fields, fields), :]
        return carry

    lax.fori_loop(0, total // group_size, place, 0)


def local_fluxes(rows_from, rows_to, local_pairs, table, fields, nodes, elems):
    total = rows_from.shape[0]
    vmem = pl.BlockSpec(memory_space=pltpu.VMEM)
    smem = pl.BlockSpec(memory_space=pltpu.SMEM)
    return pl.pallas_call(
        functools.partial(local_kernel, fields=fields, nodes=nodes),
        out_shape=jax.ShapeDtypeStruct((6 * elems * fields, LANES), jnp.float32),
        in_specs=[smem, smem, vmem, vmem],
        out_specs=vmem,
        scratch_shapes=[
            pltpu.VMEM((total * (fields + 1), LANES), jnp.float32),
            pltpu.VMEM((total, LANES), jnp.int32),
            pltpu.VMEM((total * fields, LANES), jnp.float32),
        ],
        compiler_params=pltpu.CompilerParams(vmem_limit_bytes=8 * MIB),
        cost_estimate=pl.CostEstimate(flops=10**7, bytes_accessed=12 * 10**6, transcendentals=0),
        name="local_fluxes",
    )(rows_from, rows_to, local_pairs, table)


def volume_kernel(
    p_ref, rs_ref, g_ref, fwd_ref, back_ref, map_ref, out_ref, sums_ref, one, two, three, four, modes, *, derivative, ramp
):
    fields, nodes = p_ref.shape[0], p_ref.shape[1]
    rows = nodes**3
    block = back_ref.shape[0]
    planes = block // (nodes * nodes)
    back = derivative.T
    lanes_here = pl.ds(pl.multiple_of(pl.program_id(0) * LANES, LANES), LANES)

    def both(at, read):
        return jnp.concatenate([read(f).reshape(rows, LANES)[at * block : (at + 1) * block] for f in range(fields)], axis=1)

    for at in range(rows // block):
        head, tail = split(both(at, lambda f: p_ref[f, :, :, :, lanes_here]))
        slopes = mxu(fwd_ref[...], jnp.concatenate([head, tail, head], axis=0))
        for f in range(fields):
            lanes = slice(f * LANES, (f + 1) * LANES)
            here = slice(at * planes, (at + 1) * planes)
            two[f, here] = slopes[:block, lanes].reshape(planes, nodes, nodes, LANES)
            three[f, here] = slopes[block:, lanes].reshape(planes, nodes, nodes, LANES)
    for f in range(fields):
        for j in range(nodes):
            slopes = derive(derivative, [p_ref[f, k, j, :, lanes_here] for k in range(nodes)])
            for i in range(nodes):
                one[f, i, j] = slopes[i]
    for i in range(nodes):
        for j in range(nodes):
            xx, yy, zz, xy, xz, yz = [g_ref[c, i, j, :, lanes_here] for c in range(6)]
            for f in range(fields):
                s1, s2, s3 = one[f, i, j], two[f, i, j], three[f, i, j]
                one[f, i, j] = xx * s1 + xy * s2 + xz * s3
                two[f, i, j] = xy * s1 + yy * s2 + yz * s3
                three[f, i, j] = xz * s1 + yz * s2 + zz * s3
    for at in range(rows // block):
        head2, tail2 = split(both(at, lambda f: two[f]))
        head3, tail3 = split(both(at, lambda f: three[f]))
        sums = mxu(back_ref[...], jnp.concatenate([head2, tail2, head2, head3, tail3, head3], axis=0))
        for f in range(fields):
            lanes = slice(f * LANES, (f + 1) * LANES)
            here = slice(at * planes, (at + 1) * planes)
            four[f, here] = rs_ref[f, here, :, :, lanes_here] - sums[:, lanes].reshape(planes, nodes, nodes, LANES)
    for f in range(fields):
        for j in range(nodes):
            sums = derive(back, [one[f, k, j] for k in range(nodes)])
            for i in range(nodes):
                out_ref[f, i, j, :, lanes_here] = four[f, i, j] - sums[i]
        restrict_nodes(lambda i, j, f=f: out_ref[f, i, j, :, lanes_here], modes, f * 8, ramp, nodes)
    hot = cell_mask(map_ref[...], sums_ref.shape[1])
    across = (((1,), (1,)), ((), ()))
    head, rest, tail = three_parts(modes[...])
    total = mxu(head, hot, across) + mxu(rest, hot, across) + mxu(tail, hot, across)

    @pl.when(pl.program_id(0) == 0)
    def _():
        sums_ref[...] = total

    @pl.when(pl.program_id(0) > 0)
    def _():
        sums_ref[...] += total


def volume(pressure, right_side, geometry, cell_row, cells, derivative, ramp):
    fields, nodes, elems = pressure.shape[0], pressure.shape[1], pressure.shape[-1]
    block = 256
    planes = block // (nodes * nodes)
    eye = np.eye(nodes)
    middle = np.kron(np.eye(planes), np.kron(derivative, eye))
    minor = np.kron(np.eye(planes), np.kron(eye, derivative))

    def parts(matrix):
        whole = jnp.asarray(matrix, jnp.float32)
        head = whole.astype(jnp.bfloat16)
        return head, (whole - head.astype(jnp.float32)).astype(jnp.bfloat16)

    head, tail = parts(np.concatenate([middle, minor], axis=0))
    forward = jnp.concatenate([head, head, tail], axis=1)
    (head2, tail2), (head3, tail3) = parts(middle.T), parts(minor.T)
    backward = jnp.concatenate([head2, head2, tail2, head3, head3, tail3], axis=1)
    whole = (fields, nodes, nodes, nodes, LANES)
    vmem = pl.BlockSpec(memory_space=pltpu.VMEM)
    return pl.pallas_call(
        functools.partial(volume_kernel, derivative=derivative, ramp=ramp),
        out_shape=(
            jax.ShapeDtypeStruct(pressure.shape, jnp.float32),
            jax.ShapeDtypeStruct((fields * 8, cells), jnp.float32),
        ),
        grid=(elems // LANES,),
        in_specs=[vmem] * 5 + [pl.BlockSpec((1, LANES), lambda s: (0, s))],
        out_specs=(vmem, vmem),
        scratch_shapes=[pltpu.VMEM(whole, jnp.float32)] * 4 + [pltpu.VMEM((fields * 8, LANES), jnp.float32)],
        compiler_params=pltpu.CompilerParams(vmem_limit_bytes=14 * MIB),
        cost_estimate=pl.CostEstimate(flops=10**9, bytes_accessed=13 * 10**6, transcendentals=0),
    )(pressure, right_side, geometry, forward, backward, cell_row)


def center_kernel(
    to_ref, slots_ref, own_ref, up_ref, down_ref, right_ref, left_ref, rows_in, rows_ref, order, result, *, fields, nodes
):
    cap = to_ref.shape[0] // 9
    del rows_in
    sources = {1: (down_ref, 0), 3: (left_ref, 1), 5: (right_ref, 1), 7: (up_ref, 0)}
    cross_flags(slots_ref, order)
    cross_rows(sources, own_ref, order, result, cap, fields, nodes)
    put_blocks(sources, to_ref, result, rows_ref, cap, fields)


def center_rows(rows_to, slots, own, near, local_rows, fields, nodes):
    slot_total = rows_to.shape[0]
    padded = -(-slot_total // LANES) * LANES
    vmem = pl.BlockSpec(memory_space=pltpu.VMEM)
    return pl.pallas_call(
        functools.partial(center_kernel, fields=fields, nodes=nodes),
        out_shape=(
            jax.ShapeDtypeStruct(local_rows.shape, jnp.float32),
            jax.ShapeDtypeStruct((padded, LANES), jnp.int32),
        ),
        in_specs=[pl.BlockSpec(memory_space=pltpu.SMEM)] + [vmem] * 7,
        out_specs=(vmem, vmem),
        scratch_shapes=[pltpu.VMEM((slot_total * fields, LANES), jnp.float32)],
        input_output_aliases={7: 0},
        compiler_params=pltpu.CompilerParams(vmem_limit_bytes=8 * MIB),
        cost_estimate=pl.CostEstimate(flops=10**7, bytes_accessed=10**6, transcendentals=0),
        name="center_rows",
    )(rows_to, slots, own, *near, local_rows)


def cross_kernel(
    to_ref, order, own_ref, far_up, far_down, rows_in, map_ref, base_ref, table_ref,
    rows_ref, sums_ref, result, *, elems, fields, nodes,
):
    slot_total = to_ref.shape[0]
    cap = slot_total // 9
    del rows_in
    sources = {8: (far_up, 0), 6: (far_up, 1), 2: (far_down, 0), 0: (far_down, 1)}
    cross_rows(sources, own_ref, order, result, cap, fields, nodes)
    put_blocks(sources, to_ref, result, rows_ref, cap, fields)
    across = (((1,), (1,)), ((), ()))
    values = []
    for f in range(fields):
        parts = [split(rows_ref[pl.ds(face * elems * fields + f, elems, stride=fields), :]) for face in range(6)]
        by_head = mxu(table_ref[...], jnp.concatenate([head for head, _ in parts], axis=1), across)
        by_tail = mxu(table_ref[...], jnp.concatenate([tail for _, tail in parts], axis=1), across)
        values.append(by_head[:8] + by_head[8:] + by_tail[:8])
    hot = cell_mask(map_ref[...], base_ref.shape[1])
    head, rest, tail = three_parts(jnp.concatenate(values, axis=0))
    sums_ref[...] = base_ref[...] - (mxu(head, hot, across) + mxu(rest, hot, across) + mxu(tail, hot, across))


def cross_sums(rows_to, flags, own, far, local_rows, cell_row, base, derivative, prolong, nodes):
    elems = cell_row.shape[1]
    fields = base.shape[0] // 8
    slot_total = rows_to.shape[0]
    table = jnp.asarray(face_modes(derivative, prolong).reshape(-1, 8).T, jnp.float32)
    head = table.astype(jnp.bfloat16)
    both = jnp.concatenate([head, (table - head.astype(jnp.float32)).astype(jnp.bfloat16)], axis=0)
    vmem = pl.BlockSpec(memory_space=pltpu.VMEM)
    return pl.pallas_call(
        functools.partial(cross_kernel, elems=elems, fields=fields, nodes=nodes),
        out_shape=(
            jax.ShapeDtypeStruct(local_rows.shape, jnp.float32),
            jax.ShapeDtypeStruct(base.shape, jnp.float32),
        ),
        in_specs=[pl.BlockSpec(memory_space=pltpu.SMEM)] + [vmem] * 8,
        out_specs=(vmem, vmem),
        scratch_shapes=[pltpu.VMEM((slot_total * fields, LANES), jnp.float32)],
        input_output_aliases={5: 0},
        compiler_params=pltpu.CompilerParams(vmem_limit_bytes=12 * MIB),
        cost_estimate=pl.CostEstimate(flops=10**8, bytes_accessed=4 * 10**6, transcendentals=0),
        name="cross_sums",
    )(rows_to, flags, own, *far, local_rows, cell_row, base, both)


def lift_kernel(start_ref, rows_ref, *refs, derivative, elems, first):
    res_ref, nat = refs[-2:]
    fields, nodes = res_ref.shape[0], res_ref.shape[1]
    half = nodes * nodes
    last = nodes - 1
    base = (pl.program_id(0) + first) * LANES
    here = pl.ds(pl.multiple_of(base, LANES), LANES)
    for f in range(fields):
        for face in range(6):
            nat[f, face] = rows_ref[pl.ds((face * elems + base) * fields + f, LANES, stride=fields), :].T
    value_low = column([1.0] + [0.0] * last)
    value_high = column([0.0] * last + [1.0])
    lift_low = column(list(-derivative[0]))
    lift_high = column(list(derivative[last]))
    for f in range(fields):
        for i in range(nodes):
            for j in range(nodes):
                value = start_ref[f, i, j, :, here]
                at_j = slice(j * nodes, (j + 1) * nodes)
                at_i = slice(i * nodes, (i + 1) * nodes)
                low_j = slice(half + j * nodes, half + (j + 1) * nodes)
                low_i = slice(half + i * nodes, half + (i + 1) * nodes)
                if i == 0:
                    value = value - nat[f, 0, at_j]
                if i == last:
                    value = value - nat[f, 1, at_j]
                value = value + float(derivative[0, i]) * nat[f, 0, low_j]
                value = value - float(derivative[last, i]) * nat[f, 1, low_j]
                if j == 0:
                    value = value - nat[f, 2, at_i]
                if j == last:
                    value = value - nat[f, 3, at_i]
                value = value + float(derivative[0, j]) * nat[f, 2, low_i]
                value = value - float(derivative[last, j]) * nat[f, 3, low_i]
                node = i * nodes + j
                value = value - value_low * nat[f, 4, node : node + 1]
                value = value - lift_low * nat[f, 4, half + node : half + node + 1]
                value = value - value_high * nat[f, 5, node : node + 1]
                value = value - lift_high * nat[f, 5, half + node : half + node + 1]
                res_ref[f, i, j] = value


def lift(start, rows, derivative, first, steps, earlier=()):
    fields, nodes, elems = start.shape[0], start.shape[1], start.shape[-1]
    vmem = pl.BlockSpec(memory_space=pltpu.VMEM)
    return pl.pallas_call(
        functools.partial(lift_kernel, derivative=derivative, elems=elems, first=first),
        out_shape=jax.ShapeDtypeStruct(start.shape, jnp.float32),
        grid=(steps,),
        in_specs=[vmem, vmem] + [pl.BlockSpec(memory_space=pl.ANY)] * len(earlier),
        out_specs=pl.BlockSpec((fields, nodes, nodes, nodes, LANES), lambda s: (0, 0, 0, 0, s + first)),
        scratch_shapes=[pltpu.VMEM((fields, 6, LANES, LANES), jnp.float32)],
        input_output_aliases={2: 0} if earlier else {},
        compiler_params=pltpu.CompilerParams(vmem_limit_bytes=6 * MIB),
        cost_estimate=pl.CostEstimate(flops=10**8, bytes_accessed=9 * 10**6, transcendentals=0),
    )(start, rows, *earlier)


def send_out(buffer, out_hbm, sems, step, f):
    cuts = sems.shape[2]
    size = buffer.shape[2] // cuts
    lanes = pl.ds(step * LANES if isinstance(step, int) else pl.multiple_of(step * LANES, LANES), LANES)
    return [
        pltpu.make_async_copy(
            buffer.at[step, f, cut * size : (cut + 1) * size],
            out_hbm.at[f, cut * size : (cut + 1) * size, :, :, lanes],
            sems.at[step, f, cut],
        )
        for cut in range(cuts)
    ]


def correct_kernel(p_ref, inverse_ref, map_ref, *refs, prolong, parts):
    sum_refs = refs[:parts]
    out_hbm, heads, rests, tails, buffer, sems = refs[parts:]
    step = pl.program_id(0)
    fields, nodes = p_ref.shape[0], p_ref.shape[1]
    here = pl.ds(pl.multiple_of(step * LANES, LANES), LANES)
    cells = inverse_ref.shape[-1]

    @pl.when(step == 0)
    def _():
        total = sum_refs[0][...]
        for ref in sum_refs[1:]:
            total = total + ref[...]
        for f in range(fields):
            running = None
            for j in range(8):
                term = inverse_ref[j] * total[f * 8 + j : f * 8 + j + 1, :]
                running = term if running is None else running + term
            head, rest = split(running)
            tail = (running - head.astype(jnp.float32) - rest.astype(jnp.float32)).astype(jnp.bfloat16)
            heads[f * 8 : f * 8 + 8] = head.astype(jnp.float32)
            rests[f * 8 : f * 8 + 8] = rest.astype(jnp.float32)
            tails[f * 8 : f * 8 + 8] = tail.astype(jnp.float32)

    hot = (lax.broadcasted_iota(jnp.int32, (cells, LANES), 0) == map_ref[...]).astype(jnp.bfloat16)
    spread = (
        mxu(heads[...].astype(jnp.bfloat16), hot)
        + mxu(rests[...].astype(jnp.bfloat16), hot)
        + mxu(tails[...].astype(jnp.bfloat16), hot)
    )
    ramp = prolong[:, 1]
    ramp_rows = column(list(ramp))
    for f in range(fields):
        quad = []
        for ab in range(4):
            at = f * 8 + 2 * ab
            down, up = spread[at : at + 1, :], spread[at + 1 : at + 2, :]
            quad.append(down + ramp_rows * (up - down))
        for j in range(nodes):
            down = quad[0] + float(ramp[j]) * (quad[1] - quad[0])
            slope = quad[2] + float(ramp[j]) * (quad[3] - quad[2]) - down
            for i in range(nodes):
                buffer[step, f, i, j] = p_ref[f, i, j, :, here] + (down + float(ramp[i]) * slope)
        for copy in send_out(buffer, out_hbm, sems, step, f):
            copy.start()

    @pl.when(step == pl.num_programs(0) - 1)
    def _():
        for at in range(buffer.shape[0]):
            for f in range(fields):
                for copy in send_out(buffer, out_hbm, sems, at, f):
                    copy.wait()


def corrected_field(pressure, coarse_inverse, cell_row, sums, prolong):
    fields, nodes, elems = pressure.shape[0], pressure.shape[1], pressure.shape[-1]
    cells = coarse_inverse.shape[-1]
    sum_spec = pl.BlockSpec((fields * 8, cells), lambda s: (0, 0))
    return pl.pallas_call(
        functools.partial(correct_kernel, prolong=prolong, parts=len(sums)),
        out_shape=jax.ShapeDtypeStruct(pressure.shape, jnp.float32),
        grid=(elems // LANES,),
        in_specs=[
            pl.BlockSpec(memory_space=pltpu.VMEM),
            pl.BlockSpec(coarse_inverse.shape, lambda s: (0, 0, 0)),
            pl.BlockSpec((1, LANES), lambda s: (0, s)),
        ]
        + [sum_spec] * len(sums),
        out_specs=pl.BlockSpec(memory_space=pl.ANY),
        scratch_shapes=[pltpu.VMEM((fields * 8, cells), jnp.float32)] * 3
        + [
            pltpu.VMEM((elems // LANES, fields, nodes, nodes, nodes, LANES), jnp.float32),
            pltpu.SemaphoreType.DMA((elems // LANES, fields, 4)),
        ],
        compiler_params=pltpu.CompilerParams(vmem_limit_bytes=6 * MIB),
        cost_estimate=pl.CostEstimate(flops=10**8, bytes_accessed=5 * 10**6, transcendentals=0),
        name="correct",
    )(pressure, coarse_inverse, cell_row, *sums)


def solution(mesh):
    sub_count = mesh.shape["sub"]

    def ring(axis, step):
        count = mesh.shape[axis]
        return axis, [((at + step) % count, at) for at in range(count)]

    def swap(value, axis, step):
        return lax.ppermute(value, *ring(axis, step))

    def both_ways(to_next, to_last, axis, paired):
        count = mesh.shape[axis]
        if count % 2 or not paired:
            return swap(to_last, axis, 1), swap(to_next, axis, -1)
        even = lax.axis_index(axis) % 2 == 0
        one = lax.ppermute(jnp.where(even, to_next, to_last), axis, [(at, at ^ 1) for at in range(count)])
        pairs = [(at, (at + (1 if at % 2 else -1)) % count) for at in range(count)]
        two = lax.ppermute(jnp.where(even, to_last, to_next), axis, pairs)
        return jnp.where(even, one, two), jnp.where(even, two, one)

    def on_device(
        pressure,
        right_side,
        geometry,
        face_weight,
        face_metric,
        cross_slots,
        local_pairs,
        coarse_map,
        coarse_inverse,
    ):
        fields, nodes, elems = pressure.shape[0], pressure.shape[1], pressure.shape[-1]
        derivative = derivative_matrix(nodes)
        points = node_points()
        prolong = np.stack([(1.0 - points) / 2.0, (1.0 + points) / 2.0], axis=1)
        cells = coarse_inverse.shape[-1]
        cell_row = coarse_map.reshape(1, elems)
        cross = cross_slots[1, 0] * elems + cross_slots[0, 0]
        pairs = jnp.concatenate(
            [local_pairs[1] * elems + local_pairs[0], local_pairs[3] * elems + local_pairs[2]]
        )
        width = fields + 1
        table, send = traces(
            cross * width,
            pltpu.with_memory_space_constraint(pressure, pltpu.HBM),
            pltpu.with_memory_space_constraint(jnp.transpose(face_weight, (1, 0, 2)), pltpu.HBM),
            pltpu.with_memory_space_constraint(jnp.transpose(face_metric, (1, 0, 2)), pltpu.HBM),
            derivative,
        )
        size = send.shape[0] // 9
        block = [send[k * size : (k + 1) * size] for k in range(9)]
        right, left = both_ways(
            jnp.concatenate([block[2], block[5], block[8]]),
            jnp.concatenate([block[0], block[3], block[6]]),
            "sub",
            False,
        )
        up, down = both_ways(block[7], block[1], "blk", True)
        steps = elems // LANES
        far_up, far_down = both_ways(
            jnp.concatenate([right[2 * size :], left[2 * size :]]),
            jnp.concatenate([right[:size], left[:size]]),
            "blk",
            True,
        )
        local_rows = local_fluxes(pairs * width, pairs * fields, local_pairs, table, fields, nodes, elems)
        start, sums = volume(pressure, right_side, geometry, cell_row, cells, derivative, prolong[:, 1])
        local_rows, flags = center_rows(
            cross * fields, cross_slots, send, (up, down, right, left), local_rows, fields, nodes
        )
        rows, sums = cross_sums(
            cross * fields,
            flags,
            send,
            (far_up, far_down),
            local_rows,
            cell_row,
            sums,
            derivative,
            prolong,
            nodes,
        )
        if sub_count == 4 and steps > 1:
            other = lax.ppermute(sums, "sub", [(at, at ^ 1) for at in range(sub_count)])
            first = max(1, steps // 4)
            residual = lift(start, rows, derivative, 0, first)
            sums = sums + other
            other = lax.ppermute(sums, "sub", [(at, at ^ 2) for at in range(sub_count)])
            residual = lift(start, rows, derivative, first, steps - first, (residual,))
            all_sums = [sums, other]
        else:
            all_sums = [sums] + [swap(sums, "sub", step) for step in range(1, sub_count)]
            residual = lift(start, rows, derivative, 0, steps)
        return residual, corrected_field(pressure, coarse_inverse, cell_row, all_sums, prolong)

    split_elems = ("blk", "sub")
    field_spec = P(None, None, None, None, split_elems)

    return jax.shard_map(
        on_device,
        mesh=mesh,
        in_specs=(
            field_spec,
            field_spec,
            field_spec,
            P(None, None, split_elems),
            P(None, None, split_elems),
            P(None, split_elems, None),
            P(None, split_elems),
            P(split_elems),
            P(None, None, "blk"),
        ),
        out_specs=(field_spec, field_spec),
        check_vma=False,
    )
```
